32 devices in a mesh: day: 2 (over x), row: 16 (over z, y, core).
Axes of the slice: x: 2, y: 2, z: 4, core: 2. Of those that a mesh axis runs over, the one named last changes fastest.
Arguments:
- spectra: bfloat16 [4096, 2, 2, 4096], P(('day', 'row')), parts along dimension 0, may hold values from -110 to 110
- pair_channels: int32 [64, 128, 2], P('row'), may hold values from 0 to 2047, as said below
- pair_live: int32 [64, 128], P('row'), may hold values from 0 to 1, as said below
Outputs:
- correlations: float32 [128, 128, 512], P(('day', 'row')), parts along dimension 0
The draws below stay inside these ranges and needn't reach their ends.
There are 2 independent parts, one for each index of `day`. The reference program is written for one: setup_inputs(seed, part) draws one part's arguments, and reference() takes and returns one part's arrays. A program takes and returns all parts, laid end to end along the dimension named above; an argument that names none is the same for every part. Nothing has to cross between parts.
Inputs may be any that keep to these rules, and one draw needn't show every extreme that they name: `pair_channels`: pair slots of device i of row are tiles i * 4 to (i + 1) * 4 - 1; their first channels are that device's own channels i * 128 to (i + 1) * 128 - 1, and their second channels lie within 128 channels of the first; distances of exactly 128 occur on both sides. `pair_live`: in each device's pair slots (tile by tile, pair by pair) the live slots come first and the padding after; every device has 128 live slots or more, and one device's slots are all live.
All inputs are finite; a program needn't handle non-finite values.
Results may differ from the reference program's by a relative error of at most 0.003.
Values may be sent and summed in bfloat16 or wider, within the bound.
A program may use at most 192 MiB of HBM per device.

```python
import math
import jax
import jax.numpy as jnp
from jax import lax

CH_DEV = 128
TILE_SLOTS = 4
WIN = 2
FREQ = 4096
BAND = 64
LAGS = 512
BLOCK = 128
HALO = 128
CHANNELS = 2048
TILES = 64


def pair_tables(key):
    device_count = TILES // TILE_SLOTS
    per_device = TILE_SLOTS * BLOCK
    base_key = jax.random.fold_in(key, 7)
    first_key, offset_key, count_key, full_key = jax.random.split(base_key, 4)
    own_offset = jax.random.randint(first_key, (device_count, per_device), 0, CH_DEV)
    reach_chan = jax.random.randint(offset_key, (device_count, per_device), -HALO, HALO + 1)
    own_offset = own_offset.at[:, 0].set(0).at[:, 1].set(CH_DEV - 1)
    reach_chan = reach_chan.at[:, 0].set(-HALO).at[:, 1].set(HALO)
    device_rows = jnp.arange(device_count, dtype=jnp.int32)[:, None]
    first_chan = device_rows * CH_DEV + own_offset
    second_chan = first_chan + reach_chan
    outside = (second_chan < 0) | (second_chan >= CHANNELS)
    second_chan = jnp.where(outside, first_chan - reach_chan, second_chan)
    live_count = jax.random.randint(count_key, (device_count,), BLOCK, per_device * 3 // 4 + 1)
    full_device = jax.random.randint(full_key, (), 0, device_count)
    live_count = jnp.where(jnp.arange(device_count) == full_device, per_device, live_count)
    live_mask = (jnp.arange(per_device)[None, :] < live_count[:, None]).astype(jnp.int32)
    pair_table = jnp.stack([first_chan, second_chan], axis=-1).reshape(TILES, BLOCK, 2)
    return (pair_table.astype(jnp.int32), live_mask.reshape(TILES, BLOCK))


def draw_pair_channels(key, part):
    return pair_tables(key)[0]


def draw_pair_live(key, part):
    return pair_tables(key)[1]


def draw_spectra(key, part):
    key_list = jax.random.split(jax.random.fold_in(key, 11), 5)
    position = jnp.arange(CHANNELS, dtype=jnp.float32) / (CHANNELS - 1)
    coupling = (1.0 + 2.0 * position) * jnp.exp(jax.random.uniform(key_list[0], (CHANNELS,), minval=-0.5, maxval=0.5))
    bin_scale = jnp.exp(jax.random.uniform(key_list[1], (FREQ,), minval=math.log(0.3), maxval=math.log(3.0)))
    shape_all = (CHANNELS, WIN, 2, FREQ)
    row_scale = jnp.exp(jax.random.uniform(key_list[2], (CHANNELS,), minval=math.log(0.3), maxval=math.log(3.0)))
    common = jnp.clip(jax.random.normal(key_list[3], (WIN, 2, FREQ)), -5.0, 5.0)
    noise_part = jnp.clip(jax.random.normal(key_list[4], shape_all), -5.0, 5.0)
    values = coupling[:, None, None, None] * common[None] + 0.6 * row_scale[:, None, None, None] * noise_part
    return (values * bin_scale).astype(jnp.bfloat16)


def setup_inputs(seed: int = 0, part: int = 0) -> dict:
    key_of = jax.random.split(jax.random.key(seed), 4)
    part_keys = jax.random.split(jax.random.fold_in(key_of[3], part), 4)
    spectra = draw_spectra(jax.random.fold_in(jax.random.fold_in(key_of[3], part), 71), part)
    pair_channels = draw_pair_channels(jax.random.fold_in(key_of[3], 71), part)
    pair_live = draw_pair_live(jax.random.fold_in(key_of[3], 71), part)
    return {"spectra": spectra, "pair_channels": pair_channels, "pair_live": pair_live}


def build_table(bin_total, lag_total):
    bin_index = jnp.arange(bin_total, dtype=jnp.int32)[:, None]
    shifts = jnp.arange(lag_total, dtype=jnp.int32)[None, :] - lag_total // 2
    phase_int = jnp.mod(bin_index * shifts, 2 * bin_total)
    angle_rad = phase_int.astype(jnp.float32) * (math.pi / bin_total)
    return jnp.concatenate([jnp.cos(angle_rad), -jnp.sin(angle_rad)], axis=0).astype(jnp.bfloat16)

def whiten(raw_rows, common):
    removed = raw_rows.astype(jnp.float32) - common[None]
    magnitude = jnp.sqrt(removed[:, :, 0] ** 2 + removed[:, :, 1] ** 2)
    row_count, window_count, bin_count = magnitude.shape
    banded = magnitude.reshape(row_count, window_count, bin_count // BAND, BAND)
    band_level = lax.optimization_barrier(jnp.mean(banded, axis=3, keepdims=True)) + 1e-06
    scaled = removed.reshape(row_count, window_count, 2, bin_count // BAND, BAND) / band_level[:, :, None]
    return scaled.reshape(raw_rows.shape).astype(jnp.bfloat16)

def cross_rows(first_rows, second_rows):
    first_f32 = first_rows.astype(jnp.float32)
    second_f32 = second_rows.astype(jnp.float32)
    real_part = lax.optimization_barrier(jnp.sum(first_f32[:, :, 0] * second_f32[:, :, 0] + first_f32[:, :, 1] * second_f32[:, :, 1], axis=1))
    imag_part = lax.optimization_barrier(jnp.sum(first_f32[:, :, 1] * second_f32[:, :, 0] - first_f32[:, :, 0] * second_f32[:, :, 1], axis=1))
    return jnp.concatenate([real_part, imag_part], axis=1).astype(jnp.bfloat16)

def reference(spectra, pair_channels, pair_live):
    common = lax.optimization_barrier(jnp.sum(spectra, axis=0, dtype=jnp.float32)) / CHANNELS
    whitened = whiten(spectra, common)
    lag_matrix = build_table(FREQ, LAGS)
    norm_factor = 1.0 / math.sqrt(FREQ * WIN)

    def one_tile(operands):
        tile_pairs, tile_live = operands
        products = cross_rows(whitened[tile_pairs[:, 0]], whitened[tile_pairs[:, 1]])
        summed = jnp.dot(products, lag_matrix, preferred_element_type=jnp.float32)
        return summed * norm_factor * tile_live.astype(jnp.float32)[:, None]
    return lax.map(one_tile, (pair_channels, pair_live))
```

```python
import functools
import math

import jax
import jax.numpy as jnp
from jax import lax
from jax.experimental import pallas as pl
from jax.experimental.pallas import tpu as pltpu
from jax.sharding import PartitionSpec as P

BAND = 64
LAGS = 512
LANES = 128
SLAB = 8 * LANES
PIECES = 4
WHITEN_ROWS = 64
UNROLL = 16
EARLY = 2
MESH = pl.DeviceIdType.MESH


def kernel(count, windows, norm_factor, own_hbm, pairs_ref, live_ref, out_ref,
           own, beside, across, white, spread, planes, lag, acc, base, turn,
           sums, heard_half, red, heard, other_half, common,
           far_pairs, far_live, tab_v, tab_a0, tab_b0, tab_a1, tab_b1, back_out, back_in,
           load_sem, beside_send, beside_recv, across_send, across_recv, sum_send, sum_recv,
           tab_send, tab_recv, back_send, back_recv, smem_sem):
    slabs, rows = own.shape[:2]
    half = slabs // 2
    span = windows * 16
    bins = slabs * SLAB
    pairs = out_ref.shape[0]
    me = lax.axis_index("row")
    core = lax.rem(me, 2)
    partner = me + 1 - 2 * core
    rounds = count.bit_length() - 1
    channels = count * rows
    piece = rows // PIECES
    gets = (core == 1) & (me < count - 1)
    gives = (core == 0) & (me > 0)
    right, left = lax.rem(me + 1, count), lax.rem(me + count - 1, count)
    near = jnp.where(core == 1, right, left)
    zero_row = 3 * rows

    def remote(src, dst, sent, got, target):
        return pltpu.make_async_remote_copy(
            src_ref=src, dst_ref=dst, send_sem=sent, recv_sem=got,
            device_id={"row": target}, device_id_type=MESH)

    def load(q):
        return pltpu.make_async_copy(own_hbm.at[:, :, q], own.at[q], load_sem.at[q])

    def send_beside(q):
        return remote(own_hbm.at[:, :, q], beside.at[q], beside_send.at[q], beside_recv.at[q], partner)

    def send_across(q, k, target):
        at = pl.ds(pl.multiple_of(k * piece, piece), piece)
        return remote(own_hbm.at[at, :, q], across.at[q, at], across_send.at[q, k], across_recv.at[q, k], target)

    def send_tables(target):
        return (remote(pairs_ref, far_pairs, tab_send.at[0], tab_recv.at[0], target),
                remote(live_ref, far_live, tab_send.at[1], tab_recv.at[1], target))

    def send_back(target):
        return remote(back_out, back_in, back_send.at[0], back_recv.at[0], target)

    for q in range(slabs):
        load(q).start()

    barrier = pltpu.get_barrier_semaphore()
    partners = [me ^ (1 << r) for r in range(rounds)]
    for p in partners:
        pl.semaphore_signal(barrier, inc=1, device_id={"row": p}, device_id_type=MESH)

    pl.semaphore_signal(barrier, inc=1, device_id={"row": near}, device_id_type=MESH)
    pl.semaphore_wait(barrier, rounds + 1)

    @pl.when(gives)
    def _():
        for copy in send_tables(left):
            copy.start()
        for k in range(EARLY):
            send_across(0, k, left).start()

    for q in range(slabs):
        send_beside(q).start()

    acc[...] = jnp.zeros_like(acc)
    white[pl.ds(zero_row, 8)] = jnp.zeros((8,) + white.shape[1:], jnp.float32)

    for q in range(slabs):
        load(q).wait()

        def step(i, total):
            block = own[q, pl.ds(pl.multiple_of(i * 8, 8), 8)].astype(jnp.float32)
            return total + jnp.sum(block, axis=0)

        total = lax.fori_loop(0, rows // 8, step, jnp.zeros((windows, 16, LANES), jnp.float32))
        sums[q // half, pl.ds((q % half) * span, span), :] = total.reshape(span, LANES)

    copies = []

    def exchange(r, src, dst):
        copy = remote(src, dst, sum_send.at[r], sum_recv.at[r], partners[r] if r < rounds else partner)
        copy.start()
        copies.append(copy)

    exchange(0, sums.at[1 - core], heard_half)
    shifts = lax.broadcasted_iota(jnp.int32, (LANES, LAGS), 1) + (2 * bins - LAGS // 2)
    phase = lax.rem(lax.broadcasted_iota(jnp.int32, (LANES, LAGS), 0) * shifts, 2 * bins)
    angle = phase.astype(jnp.float32) * (math.pi / bins)
    base[0] = jnp.cos(angle)
    base[1] = jnp.sin(angle)
    copies[0].wait_recv()
    red[0] = sums[core] + heard_half[...]

    tiles = bins // LANES
    for r in range(1, rounds):
        exchange(r, red.at[r - 1], heard.at[r - 1])
        if r == 1:
            @pl.when(gives)
            def _():
                for k in range(EARLY, PIECES):
                    send_across(0, k, left).start()

                @pl.loop(1, slabs)
                def _(q):
                    for k in range(PIECES):
                        send_across(q, k, left).start()

            shift_row = lax.broadcasted_iota(jnp.int32, (tiles, LAGS), 1) + (2 * bins - LAGS // 2)
            turns = lax.rem(lax.broadcasted_iota(jnp.int32, (tiles, LAGS), 0) * shift_row, 2 * bins)
            turned = lax.rem(turns * LANES, 2 * bins).astype(jnp.float32) * (math.pi / bins)
            turn[0] = jnp.cos(turned)
            turn[1] = jnp.sin(turned)

        @pl.loop((r - 1) * slabs // (rounds - 1), r * slabs // (rounds - 1))
        def _(q):
            @pl.loop(0, 8)
            def _(f):
                ch = turn[0, pl.ds(q * 8 + f, 1), :]
                sh = turn[1, pl.ds(q * 8 + f, 1), :]

                @pl.loop(0, LANES // 16)
                def _(k):
                    at = pl.ds(pl.multiple_of(k * 16, 16), 16)
                    to = pl.ds(pl.multiple_of(f * LANES + k * 16, 16), 16)
                    bc, bs = base[0, at, :], base[1, at, :]
                    lag[q, 0, to, :] = (bc * ch - bs * sh).astype(jnp.bfloat16)
                    lag[q, 1, to, :] = (-(bs * ch + bc * sh)).astype(jnp.bfloat16)

        copies[r].wait_recv()
        red[r] = red[r - 1] + heard[r - 1]
    exchange(rounds, red.at[rounds - 1], other_half)

    def place(index, regions):
        slot = jnp.full_like(index, zero_row)
        for device, start in regions:
            offset = index - device * rows
            slot = jnp.where((offset >= 0) & (offset < rows), offset + start, slot)
        return slot

    first, second, live = pairs_ref[0:1], pairs_ref[1:2], live_ref[...]
    far_device = jnp.where(gets, me + 1, -2)
    regions = ((me, 0), (partner, rows), (far_device, 2 * rows))
    tab_v[0] = jnp.where(live > 0, place(first, regions), zero_row)
    tab_v[1] = place(second, regions)

    @pl.when(gets)
    def _():
        for copy in send_tables(right):
            copy.wait_recv()
        tab_v[2] = jnp.where(far_live[...] > 0, place(far_pairs[0:1], ((me + 1, 2 * rows),)), zero_row)
        tab_v[3] = place(far_pairs[1:2], ((me, 0),))

    @pl.when(jnp.logical_not(gets))
    def _():
        tab_v[2] = jnp.full((1, pairs), zero_row, jnp.int32)
        tab_v[3] = jnp.full((1, pairs), zero_row, jnp.int32)

    tables = (tab_a0, tab_b0, tab_a1, tab_b1)
    moves = [pltpu.make_async_copy(tab_v.at[i], table, smem_sem.at[i]) for i, table in enumerate(tables)]
    for move in moves:
        move.start()

    copies[rounds].wait_recv()
    per = half * windows * 8
    for r in range(2):
        common[r, pl.ds(core * half, half)] = (
            red[rounds - 1, pl.ds(r, per, stride=2), :] * (1.0 / channels)).reshape(half, windows * 8, LANES)
        common[r, pl.ds((1 - core) * half, half)] = (
            other_half[pl.ds(r, per, stride=2), :] * (1.0 / channels)).reshape(half, windows * 8, LANES)
    for move in moves:
        move.wait()

    lane_r = lax.broadcasted_iota(jnp.int32, (LANES, LANES), 0) // BAND
    lane_c = lax.broadcasted_iota(jnp.int32, (LANES, LANES), 1) // BAND
    same = (lane_r == lane_c).astype(jnp.float32).astype(jnp.bfloat16)
    size = WHITEN_ROWS
    depth = windows * 8

    def whiten(q, source, i, start):
        at = pl.ds(pl.multiple_of(i * size, size), size)
        spread[...] = source[q, at].astype(jnp.float32).reshape(size * span, LANES)
        re = spread[pl.ds(0, size * depth, stride=2), :].reshape(size, depth, LANES) - common[0, q][None]
        im = spread[pl.ds(1, size * depth, stride=2), :].reshape(size, depth, LANES) - common[1, q][None]
        power = (re * re + im * im).reshape(size * depth, LANES)
        mag = power * lax.rsqrt(jnp.maximum(power, 1e-30))
        hi = mag.astype(jnp.bfloat16)
        lo = (mag - hi.astype(jnp.float32)).astype(jnp.bfloat16)
        level = jnp.dot(hi, same, preferred_element_type=jnp.float32)
        level += jnp.dot(lo, same, preferred_element_type=jnp.float32)
        scale = (1.0 / (level * (1.0 / BAND) + 1e-06)).reshape(size, depth, LANES)
        to = pl.ds(pl.multiple_of(start + i * size, 8), size)
        wr = (re * scale).astype(jnp.bfloat16).astype(jnp.float32)
        wi = (im * scale).astype(jnp.bfloat16).astype(jnp.float32)
        white[to, 0:windows] = wr.reshape(size, windows, 8, LANES)
        white[to, windows : 2 * windows] = wi.reshape(size, windows, 8, LANES)

    def whiten_all(q, source, start):
        @pl.loop(0, rows // size)
        def _(i):
            whiten(q, source, i, start)

    def correlate(group, q):
        table_a, table_b = tables[2 * group], tables[2 * group + 1]

        @pl.loop(0, pairs // UNROLL)
        def _(i):
            at = pl.multiple_of(i * UNROLL * 8, 64)
            for u in range(UNROLL):
                p = i * UNROLL + u
                a, b = white.at[table_a[0, p]], white.at[table_b[0, p]]
                cross_re, cross_im = None, None
                for w in range(windows):
                    ar, ai, br, bi = a[w], a[windows + w], b[w], b[windows + w]
                    part_re, part_im = ar * br + ai * bi, ai * br - ar * bi
                    cross_re = part_re if cross_re is None else cross_re + part_re
                    cross_im = part_im if cross_im is None else cross_im + part_im
                to = pl.ds(at + (u // 8) * 64 + u % 8, 8, stride=8)
                planes[0, to, :] = cross_re
                planes[1, to, :] = cross_im

        total = None
        for r in range(2):
            plane = planes[r].reshape(pairs // 8, 8, 8, LANES)
            cross = jnp.concatenate([plane[:, f].reshape(pairs, LANES).astype(jnp.bfloat16) for f in range(8)], axis=1)
            part = jnp.dot(cross, lag[q, r], preferred_element_type=jnp.float32)
            total = part if total is None else total + part
        acc[group] += total

    @pl.loop(0, slabs)
    def _(q):
        whiten_all(q, own, 0)
        send_beside(q).wait_recv()
        whiten_all(q, beside, rows)

        @pl.when(gets)
        def _():
            for k in range(PIECES):
                send_across(q, k, right).wait_recv()
            whiten_all(q, across, 2 * rows)
            correlate(1, q)

            @pl.when(q == slabs - 1)
            def _():
                back_out[...] = acc[1].astype(jnp.bfloat16)
                send_back(right).start()

        correlate(0, q)

    @pl.when(gives)
    def _():
        send_back(left).wait_recv()
        acc[0] += back_in[...].astype(jnp.float32)

    out_ref[...] = acc[0] * norm_factor

    for copy in copies:
        copy.wait_send()
    for q in range(slabs):
        send_beside(q).wait_send()

    @pl.when(gives)
    def _():
        for copy in send_tables(left):
            copy.wait_send()

        @pl.loop(0, slabs)
        def _(q):
            for k in range(PIECES):
                send_across(q, k, left).wait_send()

    @pl.when(gets)
    def _():
        send_back(right).wait_send()


def body(spectra, pair_channels, pair_live):
    rows, windows, _, bins = spectra.shape
    count = lax.axis_size("row")
    slabs = bins // SLAB
    view = spectra.reshape(rows, windows, 2, bins // LANES, LANES).transpose(0, 1, 3, 2, 4)
    view = view.reshape(rows, windows, slabs, 16, LANES)
    tile_count, tile_pairs = pair_live.shape
    pairs = tile_count * tile_pairs
    index = jnp.transpose(pair_channels, (2, 0, 1)).reshape(2, pairs)
    live = pair_live.reshape(1, pairs)
    rounds = count.bit_length() - 1
    half = slabs // 2
    span = windows * 16
    vmem = pl.BlockSpec(memory_space=pltpu.VMEM)
    dma = pltpu.SemaphoreType.DMA
    f32, bf16, i32 = jnp.float32, jnp.bfloat16, jnp.int32
    raw = pltpu.VMEM((slabs, rows, windows, 16, LANES), bf16)
    result = pl.pallas_call(
        functools.partial(kernel, count, windows, 1.0 / math.sqrt(bins * windows)),
        out_shape=jax.ShapeDtypeStruct((pairs, LAGS), f32),
        in_specs=[pl.BlockSpec(memory_space=pl.ANY), vmem, vmem],
        out_specs=vmem,
        scratch_shapes=[
            raw, raw, raw,
            pltpu.VMEM((3 * rows + 8, 2 * windows, 8, LANES), f32),
            pltpu.VMEM((WHITEN_ROWS * span, LANES), f32),
            pltpu.VMEM((2, pairs * 8, LANES), f32),
            pltpu.VMEM((slabs, 2, SLAB, LAGS), bf16),
            pltpu.VMEM((2, pairs, LAGS), f32),
            pltpu.VMEM((2, LANES, LAGS), f32),
            pltpu.VMEM((2, bins // LANES, LAGS), f32),
            pltpu.VMEM((2, half * span, LANES), f32),
            pltpu.VMEM((half * span, LANES), f32),
            pltpu.VMEM((rounds, half * span, LANES), f32),
            pltpu.VMEM((rounds - 1, half * span, LANES), f32),
            pltpu.VMEM((half * span, LANES), f32),
            pltpu.VMEM((2, slabs, windows * 8, LANES), f32),
            pltpu.VMEM((2, pairs), i32),
            pltpu.VMEM((1, pairs), i32),
            pltpu.VMEM((4, 1, pairs), i32),
            pltpu.SMEM((1, pairs), i32), pltpu.SMEM((1, pairs), i32),
            pltpu.SMEM((1, pairs), i32), pltpu.SMEM((1, pairs), i32),
            pltpu.VMEM((pairs, LAGS), bf16),
            pltpu.VMEM((pairs, LAGS), bf16),
            dma((slabs,)), dma((slabs,)), dma((slabs,)), dma((slabs, PIECES)), dma((slabs, PIECES)),
            dma((rounds + 1,)), dma((rounds + 1,)), dma((2,)), dma((2,)), dma((1,)), dma((1,)), dma((4,)),
        ],
        compiler_params=pltpu.CompilerParams(
            collective_id=0, has_side_effects=True, vmem_limit_bytes=60 * 2**20),
    )(view, index, live)
    return result.reshape(tile_count, tile_pairs, LAGS)


def solution(mesh):
    placed = (P(("day", "row"), None, None, None), P("row", None, None), P("row", None))
    return jax.shard_map(
        body, mesh=mesh, in_specs=placed, out_specs=P(("day", "row"), None, None), check_vma=False
    )
```

```python
import functools
import math

import jax
import jax.numpy as jnp
from jax import lax
from jax.experimental import pallas as pl
from jax.experimental.pallas import tpu as pltpu
from jax.sharding import PartitionSpec as P

BAND = 64
LAGS = 512
LANES = 128
SLAB = 8 * LANES
PIECES = 4
WHITEN_ROWS = 64
UNROLL = 16
MESH = pl.DeviceIdType.MESH


def kernel(count, windows, norm_factor, own_hbm, pairs_ref, live_ref, out_ref,
           own, beside, across, white, spread, planes, lag, acc, base, turn,
           sums, handed, red, heard, common,
           far_pairs, far_live, tab_v, tab_a0, tab_b0, tab_a1, tab_b1, back_out, back_in,
           load_sem, beside_send, beside_recv, across_send, across_recv, sum_send, sum_recv,
           tab_send, tab_recv, back_send, back_recv, smem_sem):
    slabs, rows = own.shape[:2]
    span = windows * 16
    bins = slabs * SLAB
    pairs = out_ref.shape[0]
    me = lax.axis_index("row")
    core = lax.rem(me, 2)
    partner = me + 1 - 2 * core
    rounds = count.bit_length() - 1
    channels = count * rows
    piece = rows // PIECES
    gets = (core == 1) & (me < count - 1)
    gives = (core == 0) & (me > 0)
    right, left = lax.rem(me + 1, count), lax.rem(me + count - 1, count)
    near = jnp.where(core == 1, right, left)
    zero_row = 3 * rows

    def remote(src, dst, sent, got, target):
        return pltpu.make_async_remote_copy(
            src_ref=src, dst_ref=dst, send_sem=sent, recv_sem=got,
            device_id={"row": target}, device_id_type=MESH)

    def load(q):
        return pltpu.make_async_copy(own_hbm.at[:, :, q], own.at[q], load_sem.at[q])

    def send_beside(q):
        return remote(own_hbm.at[:, :, q], beside.at[q], beside_send.at[q], beside_recv.at[q], partner)

    def send_across(q, k, target):
        at = pl.ds(pl.multiple_of(k * piece, piece), piece)
        return remote(own_hbm.at[at, :, q], across.at[q, at], across_send.at[q, k], across_recv.at[q, k], target)

    def send_tables(target):
        return (remote(pairs_ref, far_pairs, tab_send.at[0], tab_recv.at[0], target),
                remote(live_ref, far_live, tab_send.at[1], tab_recv.at[1], target))

    def send_back(target):
        return remote(back_out, back_in, back_send.at[0], back_recv.at[0], target)

    for q in range(slabs):
        load(q).start()

    barrier = pltpu.get_barrier_semaphore()
    hops = [me ^ (1 << r) for r in range(1, rounds)]
    for p in (partner, near):
        pl.semaphore_signal(barrier, inc=1, device_id={"row": p}, device_id_type=MESH)

    @pl.when(core == 1)
    def _():
        for p in hops:
            pl.semaphore_signal(barrier, inc=1, device_id={"row": p}, device_id_type=MESH)

    pl.semaphore_wait(barrier, 2 + core * len(hops))

    @pl.when(gives)
    def _():
        for copy in send_tables(left):
            copy.start()

        @pl.loop(0, slabs)
        def _(q):
            for k in range(PIECES):
                send_across(q, k, left).start()

    for q in range(slabs):
        send_beside(q).start()

    acc[...] = jnp.zeros_like(acc)
    white[pl.ds(zero_row, 8)] = jnp.zeros((8,) + white.shape[1:], jnp.float32)

    for q in range(slabs):
        load(q).wait()

        def step(i, total):
            block = own[q, pl.ds(pl.multiple_of(i * 8, 8), 8)].astype(jnp.float32)
            return total + jnp.sum(block, axis=0)

        total = lax.fori_loop(0, rows // 8, step, jnp.zeros((windows, 16, LANES), jnp.float32))
        sums[pl.ds(q * span, span), :] = total.reshape(span, LANES)

    def hand_over():
        return remote(sums, handed, sum_send.at[0], sum_recv.at[0], partner)

    def hop(r):
        return remote(red.at[r], heard.at[r], sum_send.at[r + 1], sum_recv.at[r + 1], hops[r])

    def hand_back():
        return remote(red.at[rounds - 1], handed, sum_send.at[rounds], sum_recv.at[rounds], partner)

    @pl.when(core == 0)
    def _():
        hand_over().start()

    shifts = lax.broadcasted_iota(jnp.int32, (LANES, LAGS), 1) + (2 * bins - LAGS // 2)
    phase = lax.rem(lax.broadcasted_iota(jnp.int32, (LANES, LAGS), 0) * shifts, 2 * bins)
    angle = phase.astype(jnp.float32) * (math.pi / bins)
    base[0] = jnp.cos(angle)
    base[1] = jnp.sin(angle)

    @pl.when(core == 1)
    def _():
        hand_over().wait_recv()
        red[0] = sums[...] + handed[...]
        hop(0).start()

    tiles = bins // LANES
    shift_row = lax.broadcasted_iota(jnp.int32, (tiles, LAGS), 1) + (2 * bins - LAGS // 2)
    turns = lax.rem(lax.broadcasted_iota(jnp.int32, (tiles, LAGS), 0) * shift_row, 2 * bins)
    turned = lax.rem(turns * LANES, 2 * bins).astype(jnp.float32) * (math.pi / bins)
    turn[0] = jnp.cos(turned)
    turn[1] = jnp.sin(turned)

    for r in range(rounds - 1):
        @pl.loop(r * slabs // (rounds - 1), (r + 1) * slabs // (rounds - 1))
        def _(q):
            @pl.loop(0, 8)
            def _(f):
                ch = turn[0, pl.ds(q * 8 + f, 1), :]
                sh = turn[1, pl.ds(q * 8 + f, 1), :]

                @pl.loop(0, LANES // 16)
                def _(k):
                    at = pl.ds(pl.multiple_of(k * 16, 16), 16)
                    to = pl.ds(pl.multiple_of(f * LANES + k * 16, 16), 16)
                    bc, bs = base[0, at, :], base[1, at, :]
                    lag[q, 0, to, :] = (bc * ch - bs * sh).astype(jnp.bfloat16)
                    lag[q, 1, to, :] = (-(bs * ch + bc * sh)).astype(jnp.bfloat16)

        @pl.when(core == 1)
        def _():
            hop(r).wait_recv()
            red[r + 1] = red[r] + heard[r]
            if r + 2 < rounds:
                hop(r + 1).start()
            else:
                hand_back().start()

    def place(index, regions):
        slot = jnp.full_like(index, zero_row)
        for device, start in regions:
            offset = index - device * rows
            slot = jnp.where((offset >= 0) & (offset < rows), offset + start, slot)
        return slot

    first, second, live = pairs_ref[0:1], pairs_ref[1:2], live_ref[...]
    far_device = jnp.where(gets, me + 1, -2)
    regions = ((me, 0), (partner, rows), (far_device, 2 * rows))
    tab_v[0] = jnp.where(live > 0, place(first, regions), zero_row)
    tab_v[1] = place(second, regions)

    @pl.when(gets)
    def _():
        for copy in send_tables(right):
            copy.wait_recv()
        tab_v[2] = jnp.where(far_live[...] > 0, place(far_pairs[0:1], ((me + 1, 2 * rows),)), zero_row)
        tab_v[3] = place(far_pairs[1:2], ((me, 0),))

    @pl.when(jnp.logical_not(gets))
    def _():
        tab_v[2] = jnp.full((1, pairs), zero_row, jnp.int32)
        tab_v[3] = jnp.full((1, pairs), zero_row, jnp.int32)

    tables = (tab_a0, tab_b0, tab_a1, tab_b1)
    moves = [pltpu.make_async_copy(tab_v.at[i], table, smem_sem.at[i]) for i, table in enumerate(tables)]
    for move in moves:
        move.start()

    def set_common(total):
        for r in range(2):
            strided = total[pl.ds(r, slabs * windows * 8, stride=2), :] * (1.0 / channels)
            common[r] = strided.reshape(slabs, windows * 8, LANES)

    @pl.when(core == 1)
    def _():
        set_common(red.at[rounds - 1])

    @pl.when(core == 0)
    def _():
        hand_back().wait_recv()
        set_common(handed)

    for move in moves:
        move.wait()

    lane_r = lax.broadcasted_iota(jnp.int32, (LANES, LANES), 0) // BAND
    lane_c = lax.broadcasted_iota(jnp.int32, (LANES, LANES), 1) // BAND
    same = (lane_r == lane_c).astype(jnp.float32).astype(jnp.bfloat16)
    size = WHITEN_ROWS
    depth = windows * 8

    def whiten(q, source, i, start):
        at = pl.ds(pl.multiple_of(i * size, size), size)
        spread[...] = source[q, at].astype(jnp.float32).reshape(size * span, LANES)
        re = spread[pl.ds(0, size * depth, stride=2), :].reshape(size, depth, LANES) - common[0, q][None]
        im = spread[pl.ds(1, size * depth, stride=2), :].reshape(size, depth, LANES) - common[1, q][None]
        power = (re * re + im * im).reshape(size * depth, LANES)
        mag = power * lax.rsqrt(jnp.maximum(power, 1e-30))
        hi = mag.astype(jnp.bfloat16)
        lo = (mag - hi.astype(jnp.float32)).astype(jnp.bfloat16)
        level = jnp.dot(hi, same, preferred_element_type=jnp.float32)
        level += jnp.dot(lo, same, preferred_element_type=jnp.float32)
        scale = (1.0 / (level * (1.0 / BAND) + 1e-06)).reshape(size, depth, LANES)
        to = pl.ds(pl.multiple_of(start + i * size, 8), size)
        wr = (re * scale).astype(jnp.bfloat16).astype(jnp.float32)
        wi = (im * scale).astype(jnp.bfloat16).astype(jnp.float32)
        white[to, 0:windows] = wr.reshape(size, windows, 8, LANES)
        white[to, windows : 2 * windows] = wi.reshape(size, windows, 8, LANES)

    def whiten_all(q, source, start):
        @pl.loop(0, rows // size)
        def _(i):
            whiten(q, source, i, start)

    def correlate(group, q):
        table_a, table_b = tables[2 * group], tables[2 * group + 1]

        @pl.loop(0, pairs // UNROLL)
        def _(i):
            at = pl.multiple_of(i * UNROLL * 8, 64)
            for u in range(UNROLL):
                p = i * UNROLL + u
                a, b = white.at[table_a[0, p]], white.at[table_b[0, p]]
                cross_re, cross_im = None, None
                for w in range(windows):
                    ar, ai, br, bi = a[w], a[windows + w], b[w], b[windows + w]
                    part_re, part_im = ar * br + ai * bi, ai * br - ar * bi
                    cross_re = part_re if cross_re is None else cross_re + part_re
                    cross_im = part_im if cross_im is None else cross_im + part_im
                to = pl.ds(at + (u // 8) * 64 + u % 8, 8, stride=8)
                planes[0, to, :] = cross_re
                planes[1, to, :] = cross_im

        total = None
        for r in range(2):
            plane = planes[r].reshape(pairs // 8, 8, 8, LANES)
            cross = jnp.concatenate([plane[:, f].reshape(pairs, LANES).astype(jnp.bfloat16) for f in range(8)], axis=1)
            part = jnp.dot(cross, lag[q, r], preferred_element_type=jnp.float32)
            total = part if total is None else total + part
        acc[group] += total

    @pl.loop(0, slabs)
    def _(q):
        whiten_all(q, own, 0)
        send_beside(q).wait_recv()
        whiten_all(q, beside, rows)

        @pl.when(gets)
        def _():
            for k in range(PIECES):
                send_across(q, k, right).wait_recv()
            whiten_all(q, across, 2 * rows)
            correlate(1, q)

            @pl.when(q == slabs - 1)
            def _():
                back_out[...] = acc[1].astype(jnp.bfloat16)
                send_back(right).start()

        correlate(0, q)

    @pl.when(gives)
    def _():
        send_back(left).wait_recv()
        acc[0] += back_in[...].astype(jnp.float32)

    out_ref[...] = acc[0] * norm_factor

    for q in range(slabs):
        send_beside(q).wait_send()

    @pl.when(core == 0)
    def _():
        hand_over().wait_send()

    @pl.when(core == 1)
    def _():
        for r in range(rounds - 1):
            hop(r).wait_send()
        hand_back().wait_send()

    @pl.when(gives)
    def _():
        for copy in send_tables(left):
            copy.wait_send()

        @pl.loop(0, slabs)
        def _(q):
            for k in range(PIECES):
                send_across(q, k, left).wait_send()

    @pl.when(gets)
    def _():
        send_back(right).wait_send()


def body(spectra, pair_channels, pair_live):
    rows, windows, _, bins = spectra.shape
    count = lax.axis_size("row")
    slabs = bins // SLAB
    view = spectra.reshape(rows, windows, 2, bins // LANES, LANES).transpose(0, 1, 3, 2, 4)
    view = view.reshape(rows, windows, slabs, 16, LANES)
    tile_count, tile_pairs = pair_live.shape
    pairs = tile_count * tile_pairs
    index = jnp.transpose(pair_channels, (2, 0, 1)).reshape(2, pairs)
    live = pair_live.reshape(1, pairs)
    rounds = count.bit_length() - 1
    span = windows * 16
    vmem = pl.BlockSpec(memory_space=pltpu.VMEM)
    dma = pltpu.SemaphoreType.DMA
    f32, bf16, i32 = jnp.float32, jnp.bfloat16, jnp.int32
    raw = pltpu.VMEM((slabs, rows, windows, 16, LANES), bf16)
    result = pl.pallas_call(
        functools.partial(kernel, count, windows, 1.0 / math.sqrt(bins * windows)),
        out_shape=jax.ShapeDtypeStruct((pairs, LAGS), f32),
        in_specs=[pl.BlockSpec(memory_space=pl.ANY), vmem, vmem],
        out_specs=vmem,
        scratch_shapes=[
            raw, raw, raw,
            pltpu.VMEM((3 * rows + 8, 2 * windows, 8, LANES), f32),
            pltpu.VMEM((WHITEN_ROWS * span, LANES), f32),
            pltpu.VMEM((2, pairs * 8, LANES), f32),
            pltpu.VMEM((slabs, 2, SLAB, LAGS), bf16),
            pltpu.VMEM((2, pairs, LAGS), f32),
            pltpu.VMEM((2, LANES, LAGS), f32),
            pltpu.VMEM((2, bins // LANES, LAGS), f32),
            pltpu.VMEM((slabs * span, LANES), f32),
            pltpu.VMEM((slabs * span, LANES), f32),
            pltpu.VMEM((rounds, slabs * span, LANES), f32),
            pltpu.VMEM((rounds - 1, slabs * span, LANES), f32),
            pltpu.VMEM((2, slabs, windows * 8, LANES), f32),
            pltpu.VMEM((2, pairs), i32),
            pltpu.VMEM((1, pairs), i32),
            pltpu.VMEM((4, 1, pairs), i32),
            pltpu.SMEM((1, pairs), i32), pltpu.SMEM((1, pairs), i32),
            pltpu.SMEM((1, pairs), i32), pltpu.SMEM((1, pairs), i32),
            pltpu.VMEM((pairs, LAGS), bf16),
            pltpu.VMEM((pairs, LAGS), bf16),
            dma((slabs,)), dma((slabs,)), dma((slabs,)), dma((slabs, PIECES)), dma((slabs, PIECES)),
            dma((rounds + 1,)), dma((rounds + 1,)), dma((2,)), dma((2,)), dma((1,)), dma((1,)), dma((4,)),
        ],
        compiler_params=pltpu.CompilerParams(
            collective_id=0, has_side_effects=True, vmem_limit_bytes=60 * 2**20),
    )(view, index, live)
    return result.reshape(tile_count, tile_pairs, LAGS)


def solution(mesh):
    placed = (P(("day", "row"), None, None, None), P("row", None, None), P("row", None))
    return jax.shard_map(
        body, mesh=mesh, in_specs=placed, out_specs=P(("day", "row"), None, None), check_vma=False
    )
```

```python
import functools
import math

import jax
import jax.numpy as jnp
from jax import lax
from jax.experimental import pallas as pl
from jax.experimental.pallas import tpu as pltpu
from jax.sharding import PartitionSpec as P

BAND = 64
LAGS = 512
LANES = 128
SLAB = 8 * LANES
PIECES = 4
WHITEN_ROWS = 64
UNROLL = 16
RETURNS = 2
MESH = pl.DeviceIdType.MESH


def kernel(count, windows, norm_factor, own_hbm, pairs_ref, live_ref, out_hbm, back_in,
           own, shared, beside, across, white, spread, planes, lag, acc, base, turn,
           sums, handed, red, heard, common,
           far_pairs, far_live, tab_v, tab_a0, tab_b0, tab_a1, tab_b1, back_out,
           load_sem, beside_send, beside_recv, across_send, across_recv, sum_send, sum_recv,
           tab_send, tab_recv, back_send, back_recv, smem_sem, out_sem):
    slabs, rows = own.shape[:2]
    span = windows * 16
    bins = slabs * SLAB
    pairs = out_hbm.shape[0]
    me = lax.axis_index("row")
    core = lax.rem(me, 2)
    partner = me + 1 - 2 * core
    rounds = count.bit_length() - 1
    channels = count * rows
    piece = rows // PIECES
    gets = (core == 1) & (me < count - 1)
    gives = (core == 0) & (me > 0)
    right, left = lax.rem(me + 1, count), lax.rem(me + count - 1, count)
    near = jnp.where(core == 1, right, left)
    zero_row = 3 * rows

    def remote(src, dst, sent, got, target):
        return pltpu.make_async_remote_copy(
            src_ref=src, dst_ref=dst, send_sem=sent, recv_sem=got,
            device_id={"row": target}, device_id_type=MESH)

    def load(q):
        return pltpu.make_async_copy(own_hbm.at[:, :, q], own.at[q], load_sem.at[q])

    def send_beside(q):
        return remote(shared.at[q], beside.at[q], beside_send.at[q], beside_recv.at[q], partner)

    def send_across(q, k, target):
        at = pl.ds(pl.multiple_of(k * piece, piece), piece)
        return remote(own_hbm.at[at, :, q], across.at[q, at], across_send.at[q, k], across_recv.at[q, k], target)

    def send_tables(target):
        return (remote(pairs_ref, far_pairs, tab_send.at[0], tab_recv.at[0], target),
                remote(live_ref, far_live, tab_send.at[1], tab_recv.at[1], target))

    def send_back(t, target):
        at = pl.ds(t * (pairs // RETURNS), pairs // RETURNS)
        return remote(back_out.at[at], back_in.at[at], back_send.at[t], back_recv.at[t], target)

    for q in range(slabs):
        load(q).start()

    barrier = pltpu.get_barrier_semaphore()
    hops = [me ^ (1 << r) for r in range(1, rounds)]
    for p in (partner, near):
        pl.semaphore_signal(barrier, inc=1, device_id={"row": p}, device_id_type=MESH)

    @pl.when(core == 1)
    def _():
        for p in hops:
            pl.semaphore_signal(barrier, inc=1, device_id={"row": p}, device_id_type=MESH)

    pl.semaphore_wait(barrier, 2 + core * len(hops))

    @pl.when(gives)
    def _():
        for copy in send_tables(left):
            copy.start()

        @pl.loop(0, slabs)
        def _(q):
            for k in range(PIECES):
                send_across(q, k, left).start()

    acc[...] = jnp.zeros_like(acc)
    for h in range(2):
        white[h, pl.ds(zero_row, 8)] = jnp.zeros((8,) + white.shape[2:], jnp.float32)

    for q in range(slabs):
        load(q).wait()

        def step(i, total):
            block = own[q, pl.ds(pl.multiple_of(i * 8, 8), 8)].astype(jnp.float32)
            return total + jnp.sum(block, axis=0)

        total = lax.fori_loop(0, rows // 8, step, jnp.zeros((windows, 16, LANES), jnp.float32))
        sums[pl.ds(q * span, span), :] = total.reshape(span, LANES)

    def hand_over():
        return remote(sums, handed, sum_send.at[0], sum_recv.at[0], partner)

    def hop(r):
        return remote(red.at[r], heard.at[r], sum_send.at[r + 1], sum_recv.at[r + 1], hops[r])

    def hand_back():
        return remote(red.at[rounds - 1], handed, sum_send.at[rounds], sum_recv.at[rounds], partner)

    @pl.when(core == 0)
    def _():
        hand_over().start()

    shifts = lax.broadcasted_iota(jnp.int32, (LANES, LAGS), 1) + (2 * bins - LAGS // 2)
    phase = lax.rem(lax.broadcasted_iota(jnp.int32, (LANES, LAGS), 0) * shifts, 2 * bins)
    angle = phase.astype(jnp.float32) * (math.pi / bins)
    base[0] = jnp.cos(angle)
    base[1] = jnp.sin(angle)

    @pl.when(core == 1)
    def _():
        hand_over().wait_recv()
        red[0] = sums[...] + handed[...]
        hop(0).start()

    tiles = bins // LANES
    shift_row = lax.broadcasted_iota(jnp.int32, (tiles, LAGS), 1) + (2 * bins - LAGS // 2)
    turns = lax.rem(lax.broadcasted_iota(jnp.int32, (tiles, LAGS), 0) * shift_row, 2 * bins)
    turned = lax.rem(turns * LANES, 2 * bins).astype(jnp.float32) * (math.pi / bins)
    turn[0] = jnp.cos(turned)
    turn[1] = jnp.sin(turned)

    for r in range(rounds - 1):
        @pl.loop(r * slabs // (rounds - 1), (r + 1) * slabs // (rounds - 1))
        def _(q):
            @pl.loop(0, 8)
            def _(f):
                ch = turn[0, pl.ds(q * 8 + f, 1), :]
                sh = turn[1, pl.ds(q * 8 + f, 1), :]

                @pl.loop(0, LANES // 16)
                def _(k):
                    at = pl.ds(pl.multiple_of(k * 16, 16), 16)
                    to = pl.ds(pl.multiple_of(f * LANES + k * 16, 16), 16)
                    bc, bs = base[0, at, :], base[1, at, :]
                    lag[q, 0, to, :] = (bc * ch - bs * sh).astype(jnp.bfloat16)
                    lag[q, 1, to, :] = (-(bs * ch + bc * sh)).astype(jnp.bfloat16)

        @pl.when(core == 1)
        def _():
            hop(r).wait_recv()
            red[r + 1] = red[r] + heard[r]
            if r + 2 < rounds:
                hop(r + 1).start()
            else:
                hand_back().start()

    def place(index, regions):
        slot = jnp.full_like(index, zero_row)
        for device, start in regions:
            offset = index - device * rows
            slot = jnp.where((offset >= 0) & (offset < rows), offset + start, slot)
        return slot

    first, second, live = pairs_ref[0:1], pairs_ref[1:2], live_ref[...]
    far_device = jnp.where(gets, me + 1, -2)
    regions = ((me, 0), (partner, rows), (far_device, 2 * rows))
    tab_v[0] = jnp.where(live > 0, place(first, regions), zero_row)
    tab_v[1] = place(second, regions)

    @pl.when(gets)
    def _():
        for copy in send_tables(right):
            copy.wait_recv()
        tab_v[2] = jnp.where(far_live[...] > 0, place(far_pairs[0:1], ((me + 1, 2 * rows),)), zero_row)
        tab_v[3] = place(far_pairs[1:2], ((me, 0),))

    @pl.when(jnp.logical_not(gets))
    def _():
        tab_v[2] = jnp.full((1, pairs), zero_row, jnp.int32)
        tab_v[3] = jnp.full((1, pairs), zero_row, jnp.int32)

    tables = (tab_a0, tab_b0, tab_a1, tab_b1)
    moves = [pltpu.make_async_copy(tab_v.at[i], table, smem_sem.at[i]) for i, table in enumerate(tables)]
    for move in moves:
        move.start()

    def set_common(total):
        for r in range(2):
            strided = total[pl.ds(r, slabs * windows * 8, stride=2), :] * (1.0 / channels)
            common[r] = strided.reshape(slabs, windows * 8, LANES)

    @pl.when(core == 1)
    def _():
        set_common(red.at[rounds - 1])

    @pl.when(core == 0)
    def _():
        hand_back().wait_recv()
        set_common(handed)

    for move in moves:
        move.wait()

    lane_r = lax.broadcasted_iota(jnp.int32, (LANES, LANES), 0) // BAND
    lane_c = lax.broadcasted_iota(jnp.int32, (LANES, LANES), 1) // BAND
    same = (lane_r == lane_c).astype(jnp.float32).astype(jnp.bfloat16)
    size = WHITEN_ROWS
    depth = windows * 8

    def whiten(q, source, i, start, keep):
        at = pl.ds(pl.multiple_of(i * size, size), size)
        spread[...] = source[q, at].astype(jnp.float32).reshape(size * span, LANES)
        re = spread[pl.ds(0, size * depth, stride=2), :].reshape(size, depth, LANES) - common[0, q][None]
        im = spread[pl.ds(1, size * depth, stride=2), :].reshape(size, depth, LANES) - common[1, q][None]
        power = (re * re + im * im).reshape(size * depth, LANES)
        mag = power * lax.rsqrt(jnp.maximum(power, 1e-30))
        hi = mag.astype(jnp.bfloat16)
        lo = (mag - hi.astype(jnp.float32)).astype(jnp.bfloat16)
        level = jnp.dot(hi, same, preferred_element_type=jnp.float32)
        level += jnp.dot(lo, same, preferred_element_type=jnp.float32)
        scale = (1.0 / (level * (1.0 / BAND) + 1e-06)).reshape(size, depth, LANES)
        to = pl.ds(pl.multiple_of(start + i * size, 8), size)
        for r, part in enumerate((re, im)):
            rounded = (part * scale).astype(jnp.bfloat16)
            if keep:
                shared[q, at, r] = rounded
            wide = rounded.astype(jnp.float32).reshape(size, windows, 8, LANES)
            white[lax.rem(q, 2), to, r * windows : (r + 1) * windows] = wide

    def whiten_own(q):
        @pl.loop(0, rows // size)
        def _(i):
            whiten(q, own, i, 0, True)

        send_beside(q).start()

    def expand(q):
        @pl.loop(0, rows // 16)
        def _(i):
            at = pl.ds(pl.multiple_of(i * 16, 16), 16)
            to = pl.ds(pl.multiple_of(rows + i * 16, 16), 16)
            wide = beside[q, at].astype(jnp.float32)
            white[lax.rem(q, 2), to] = wide.reshape(16, 2 * windows, 8, LANES)

    def correlate(group, q, tile, after=None):
        table_a, table_b = tables[2 * group], tables[2 * group + 1]
        source = white.at[lax.rem(q, 2)]
        for t in range(pairs // tile):
            @pl.loop(0, tile // UNROLL)
            def _(i, t=t):
                at = pl.multiple_of(i * UNROLL * 8, 64)
                for u in range(UNROLL):
                    p = t * tile + i * UNROLL + u
                    a, b = source.at[table_a[0, p]], source.at[table_b[0, p]]
                    cross_re, cross_im = None, None
                    for w in range(windows):
                        ar, ai, br, bi = a[w], a[windows + w], b[w], b[windows + w]
                        part_re, part_im = ar * br + ai * bi, ai * br - ar * bi
                        cross_re = part_re if cross_re is None else cross_re + part_re
                        cross_im = part_im if cross_im is None else cross_im + part_im
                    to = pl.ds(at + (u // 8) * 64 + u % 8, 8, stride=8)
                    planes[0, to, :] = cross_re
                    planes[1, to, :] = cross_im

            total = None
            for r in range(2):
                plane = planes[r, 0 : tile * 8].reshape(tile // 8, 8, 8, LANES)
                cross = [plane[:, f].reshape(tile, LANES).astype(jnp.bfloat16) for f in range(8)]
                part = jnp.dot(jnp.concatenate(cross, axis=1), lag[q, r], preferred_element_type=jnp.float32)
                total = part if total is None else total + part
            if after is None:
                acc[group, t * tile : (t + 1) * tile] += total
            else:
                after(t, acc[group, t * tile : (t + 1) * tile] + total)

    def give_back(t, total):
        tile = pairs // RETURNS
        back_out[t * tile : (t + 1) * tile] = total.astype(jnp.bfloat16)
        send_back(t, right).start()

    whiten_own(0)

    @pl.loop(0, slabs)
    def _(q):
        @pl.when(q < slabs - 1)
        def _():
            whiten_own(q + 1)

        send_beside(q).wait_recv()
        expand(q)

        @pl.when(gets)
        def _():
            @pl.loop(0, rows // size)
            def _(i):
                for k in range(size // piece):
                    send_across(q, i * (size // piece) + k, right).wait_recv()
                whiten(q, across, i, 2 * rows, False)

            @pl.when(q < slabs - 1)
            def _():
                correlate(1, q, pairs)

            @pl.when(q == slabs - 1)
            def _():
                correlate(1, q, pairs // RETURNS, give_back)

        correlate(0, q, pairs)

    acc[0] = acc[0] * norm_factor
    store = pltpu.make_async_copy(acc.at[0], out_hbm, out_sem.at[0])
    store.start()

    @pl.when(gives)
    def _():
        for t in range(RETURNS):
            send_back(t, left).wait_recv()

    store.wait()
    for q in range(slabs):
        send_beside(q).wait_send()

    @pl.when(core == 0)
    def _():
        hand_over().wait_send()

    @pl.when(core == 1)
    def _():
        for r in range(rounds - 1):
            hop(r).wait_send()
        hand_back().wait_send()

    @pl.when(gives)
    def _():
        for copy in send_tables(left):
            copy.wait_send()

        @pl.loop(0, slabs)
        def _(q):
            for k in range(PIECES):
                send_across(q, k, left).wait_send()

    @pl.when(gets)
    def _():
        for t in range(RETURNS):
            send_back(t, right).wait_send()


def body(spectra, pair_channels, pair_live):
    rows, windows, _, bins = spectra.shape
    count = lax.axis_size("row")
    slabs = bins // SLAB
    view = spectra.reshape(rows, windows, 2, bins // LANES, LANES).transpose(0, 1, 3, 2, 4)
    view = view.reshape(rows, windows, slabs, 16, LANES)
    tile_count, tile_pairs = pair_live.shape
    pairs = tile_count * tile_pairs
    index = jnp.transpose(pair_channels, (2, 0, 1)).reshape(2, pairs)
    live = pair_live.reshape(1, pairs)
    rounds = count.bit_length() - 1
    span = windows * 16
    vmem = pl.BlockSpec(memory_space=pltpu.VMEM)
    dma = pltpu.SemaphoreType.DMA
    f32, bf16, i32 = jnp.float32, jnp.bfloat16, jnp.int32
    raw = pltpu.VMEM((slabs, rows, windows, 16, LANES), bf16)
    norm_factor = 1.0 / math.sqrt(bins * windows)
    result, back = pl.pallas_call(
        functools.partial(kernel, count, windows, norm_factor),
        out_shape=[jax.ShapeDtypeStruct((pairs, LAGS), f32), jax.ShapeDtypeStruct((pairs, LAGS), bf16)],
        in_specs=[pl.BlockSpec(memory_space=pl.ANY), vmem, vmem],
        out_specs=[pl.BlockSpec(memory_space=pl.ANY)] * 2,
        scratch_shapes=[
            raw,
            pltpu.VMEM((slabs, rows, 2, windows * 8, LANES), bf16),
            pltpu.VMEM((slabs, rows, 2, windows * 8, LANES), bf16),
            raw,
            pltpu.VMEM((2, 3 * rows + 8, 2 * windows, 8, LANES), f32),
            pltpu.VMEM((WHITEN_ROWS * span, LANES), f32),
            pltpu.VMEM((2, pairs * 8, LANES), f32),
            pltpu.VMEM((slabs, 2, SLAB, LAGS), bf16),
            pltpu.VMEM((2, pairs, LAGS), f32),
            pltpu.VMEM((2, LANES, LAGS), f32),
            pltpu.VMEM((2, bins // LANES, LAGS), f32),
            pltpu.VMEM((slabs * span, LANES), f32),
            pltpu.VMEM((slabs * span, LANES), f32),
            pltpu.VMEM((rounds, slabs * span, LANES), f32),
            pltpu.VMEM((rounds - 1, slabs * span, LANES), f32),
            pltpu.VMEM((2, slabs, windows * 8, LANES), f32),
            pltpu.VMEM((2, pairs), i32),
            pltpu.VMEM((1, pairs), i32),
            pltpu.VMEM((4, 1, pairs), i32),
            pltpu.SMEM((1, pairs), i32), pltpu.SMEM((1, pairs), i32),
            pltpu.SMEM((1, pairs), i32), pltpu.SMEM((1, pairs), i32),
            pltpu.VMEM((pairs, LAGS), bf16),
            dma((slabs,)), dma((slabs,)), dma((slabs,)), dma((slabs, PIECES)), dma((slabs, PIECES)),
            dma((rounds + 1,)), dma((rounds + 1,)), dma((2,)), dma((2,)), dma((RETURNS,)), dma((RETURNS,)), dma((4,)), dma((1,)),
        ],
        compiler_params=pltpu.CompilerParams(
            collective_id=0, has_side_effects=True, vmem_limit_bytes=60 * 2**20),
    )(view, index, live)
    me = lax.axis_index("row")
    gives = (me & 1) < jnp.minimum(me, 1)
    result = result + jnp.where(gives, back.astype(f32) * norm_factor, 0.0)
    return result.reshape(tile_count, tile_pairs, LAGS)


def solution(mesh):
    placed = (P(("day", "row"), None, None, None), P("row", None, None), P("row", None))
    return jax.shard_map(
        body, mesh=mesh, in_specs=placed, out_specs=P(("day", "row"), None, None), check_vma=False
    )
```

```python
import functools
import math

import jax
import jax.numpy as jnp
from jax import lax
from jax.experimental import pallas as pl
from jax.experimental.pallas import tpu as pltpu
from jax.sharding import PartitionSpec as P

BAND = 64
LAGS = 512
LANES = 128
SLAB = 8 * LANES
PIECES = 4
WHITEN_ROWS = 64
UNROLL = 16
RETURNS = 2
MESH = pl.DeviceIdType.MESH


def kernel(count, windows, norm_factor, own_hbm, pairs_hbm, live_hbm, out_hbm, back_in,
           own, shared, beside, across, white, spread, planes, lag, acc, base, turn,
           sums, handed, red, heard, common,
           near_pairs, near_live, far_pairs, far_live, tab_v, tab_a0, tab_b0, tab_a1, tab_b1, back_out,
           load_sem, beside_send, beside_recv, across_send, across_recv, sum_send, sum_recv,
           tab_load, tab_send, tab_recv, back_send, back_recv, smem_sem, out_sem):
    slabs, rows = own.shape[:2]
    span = windows * 16
    bins = slabs * SLAB
    pairs = out_hbm.shape[0]
    me = lax.axis_index("row")
    core = lax.rem(me, 2)
    partner = me + 1 - 2 * core
    rounds = count.bit_length() - 1
    channels = count * rows
    piece = rows // PIECES
    gets = (core == 1) & (me < count - 1)
    gives = (core == 0) & (me > 0)
    right, left = lax.rem(me + 1, count), lax.rem(me + count - 1, count)
    near = jnp.where(core == 1, right, left)
    zero_row = 3 * rows

    def remote(src, dst, sent, got, target):
        return pltpu.make_async_remote_copy(
            src_ref=src, dst_ref=dst, send_sem=sent, recv_sem=got,
            device_id={"row": target}, device_id_type=MESH)

    def load(q):
        return pltpu.make_async_copy(own_hbm.at[:, :, q], own.at[q], load_sem.at[q])

    def send_beside(q):
        return remote(shared.at[q], beside.at[q], beside_send.at[q], beside_recv.at[q], partner)

    def send_across(q, k, target):
        at = pl.ds(pl.multiple_of(k * piece, piece), piece)
        return remote(own_hbm.at[at, :, q], across.at[q, at], across_send.at[q, k], across_recv.at[q, k], target)

    def send_tables(target):
        return (remote(pairs_hbm, far_pairs, tab_send.at[0], tab_recv.at[0], target),
                remote(live_hbm, far_live, tab_send.at[1], tab_recv.at[1], target))

    fetches = (pltpu.make_async_copy(pairs_hbm, near_pairs, tab_load.at[0]),
               pltpu.make_async_copy(live_hbm, near_live, tab_load.at[1]))

    def send_back(t, target):
        at = pl.ds(t * (pairs // RETURNS), pairs // RETURNS)
        return remote(back_out.at[at], back_in.at[at], back_send.at[t], back_recv.at[t], target)

    for q in range(slabs):
        load(q).start()
    for fetch in fetches:
        fetch.start()

    barrier = pltpu.get_barrier_semaphore()
    hops = [me ^ (1 << r) for r in range(1, rounds)]
    for p in (partner, near):
        pl.semaphore_signal(barrier, inc=1, device_id={"row": p}, device_id_type=MESH)

    @pl.when(core == 1)
    def _():
        for p in hops:
            pl.semaphore_signal(barrier, inc=1, device_id={"row": p}, device_id_type=MESH)

    pl.semaphore_wait(barrier, 2 + core * len(hops))

    @pl.when(gives)
    def _():
        for copy in send_tables(left):
            copy.start()

        @pl.loop(0, slabs)
        def _(q):
            for k in range(PIECES):
                send_across(q, k, left).start()

    acc[...] = jnp.zeros_like(acc)
    for h in range(2):
        white[h, pl.ds(zero_row, 8)] = jnp.zeros((8,) + white.shape[2:], jnp.float32)

    for q in range(slabs):
        load(q).wait()

        def step(i, total):
            block = own[q, pl.ds(pl.multiple_of(i * 8, 8), 8)].astype(jnp.float32)
            return total + jnp.sum(block, axis=0)

        total = lax.fori_loop(0, rows // 8, step, jnp.zeros((windows, 16, LANES), jnp.float32))
        sums[pl.ds(q * span, span), :] = total.reshape(span, LANES)

    def hand_over():
        return remote(sums, handed, sum_send.at[0], sum_recv.at[0], partner)

    def hop(r):
        return remote(red.at[r], heard.at[r], sum_send.at[r + 1], sum_recv.at[r + 1], hops[r])

    def hand_back():
        return remote(red.at[rounds - 1], handed, sum_send.at[rounds], sum_recv.at[rounds], partner)

    @pl.when(core == 0)
    def _():
        hand_over().start()

    shifts = lax.broadcasted_iota(jnp.int32, (LANES, LAGS), 1) + (2 * bins - LAGS // 2)
    phase = lax.rem(lax.broadcasted_iota(jnp.int32, (LANES, LAGS), 0) * shifts, 2 * bins)
    angle = phase.astype(jnp.float32) * (math.pi / bins)
    base[0] = jnp.cos(angle)
    base[1] = jnp.sin(angle)

    @pl.when(core == 1)
    def _():
        hand_over().wait_recv()
        red[0] = sums[...] + handed[...]
        hop(0).start()

    tiles = bins // LANES
    shift_row = lax.broadcasted_iota(jnp.int32, (tiles, LAGS), 1) + (2 * bins - LAGS // 2)
    turns = lax.rem(lax.broadcasted_iota(jnp.int32, (tiles, LAGS), 0) * shift_row, 2 * bins)
    turned = lax.rem(turns * LANES, 2 * bins).astype(jnp.float32) * (math.pi / bins)
    turn[0] = jnp.cos(turned)
    turn[1] = jnp.sin(turned)

    for r in range(rounds - 1):
        @pl.loop(r * slabs // (rounds - 1), (r + 1) * slabs // (rounds - 1))
        def _(q):
            @pl.loop(0, 8)
            def _(f):
                ch = turn[0, pl.ds(q * 8 + f, 1), :]
                sh = turn[1, pl.ds(q * 8 + f, 1), :]

                @pl.loop(0, LANES // 16)
                def _(k):
                    at = pl.ds(pl.multiple_of(k * 16, 16), 16)
                    to = pl.ds(pl.multiple_of(f * LANES + k * 16, 16), 16)
                    bc, bs = base[0, at, :], base[1, at, :]
                    lag[q, 0, to, :] = (bc * ch - bs * sh).astype(jnp.bfloat16)
                    lag[q, 1, to, :] = (-(bs * ch + bc * sh)).astype(jnp.bfloat16)

        @pl.when(core == 1)
        def _():
            hop(r).wait_recv()
            red[r + 1] = red[r] + heard[r]
            if r + 2 < rounds:
                hop(r + 1).start()
            else:
                hand_back().start()

    def place(index, regions):
        slot = jnp.full_like(index, zero_row)
        for device, start in regions:
            offset = index - device * rows
            slot = jnp.where((offset >= 0) & (offset < rows), offset + start, slot)
        return slot

    for fetch in fetches:
        fetch.wait()
    first, second, live = near_pairs[0:1], near_pairs[1:2], near_live[...]
    far_device = jnp.where(gets, me + 1, -2)
    regions = ((me, 0), (partner, rows), (far_device, 2 * rows))
    tab_v[0] = jnp.where(live > 0, place(first, regions), zero_row)
    tab_v[1] = place(second, regions)

    @pl.when(gets)
    def _():
        for copy in send_tables(right):
            copy.wait_recv()
        tab_v[2] = jnp.where(far_live[...] > 0, place(far_pairs[0:1], ((me + 1, 2 * rows),)), zero_row)
        tab_v[3] = place(far_pairs[1:2], ((me, 0),))

    @pl.when(jnp.logical_not(gets))
    def _():
        tab_v[2] = jnp.full((1, pairs), zero_row, jnp.int32)
        tab_v[3] = jnp.full((1, pairs), zero_row, jnp.int32)

    tables = (tab_a0, tab_b0, tab_a1, tab_b1)
    moves = [pltpu.make_async_copy(tab_v.at[i], table, smem_sem.at[i]) for i, table in enumerate(tables)]
    for move in moves:
        move.start()

    def set_common(total):
        for r in range(2):
            strided = total[pl.ds(r, slabs * windows * 8, stride=2), :] * (1.0 / channels)
            common[r] = strided.reshape(slabs, windows * 8, LANES)

    @pl.when(core == 1)
    def _():
        set_common(red.at[rounds - 1])

    @pl.when(core == 0)
    def _():
        hand_back().wait_recv()
        set_common(handed)

    for move in moves:
        move.wait()

    lane_r = lax.broadcasted_iota(jnp.int32, (LANES, LANES), 0) // BAND
    lane_c = lax.broadcasted_iota(jnp.int32, (LANES, LANES), 1) // BAND
    same = (lane_r == lane_c).astype(jnp.float32).astype(jnp.bfloat16)
    depth = windows * 8

    def whiten(q, source, i, size, start, keep):
        at = pl.ds(pl.multiple_of(i * size, size), size)
        spread[0 : size * span] = source[q, at].astype(jnp.float32).reshape(size * span, LANES)
        re = spread[pl.ds(0, size * depth, stride=2), :].reshape(size, depth, LANES) - common[0, q][None]
        im = spread[pl.ds(1, size * depth, stride=2), :].reshape(size, depth, LANES) - common[1, q][None]
        power = (re * re + im * im).reshape(size * depth, LANES)
        mag = power * lax.rsqrt(jnp.maximum(power, 1e-30))
        hi = mag.astype(jnp.bfloat16)
        lo = (mag - hi.astype(jnp.float32)).astype(jnp.bfloat16)
        level = jnp.dot(hi, same, preferred_element_type=jnp.float32)
        level += jnp.dot(lo, same, preferred_element_type=jnp.float32)
        scale = (1.0 / (level * (1.0 / BAND) + 1e-06)).reshape(size, depth, LANES)
        to = pl.ds(pl.multiple_of(start + i * size, 8), size)
        for r, part in enumerate((re, im)):
            rounded = (part * scale).astype(jnp.bfloat16)
            if keep:
                shared[q, at, r] = rounded
            wide = rounded.astype(jnp.float32).reshape(size, windows, 8, LANES)
            white[lax.rem(q, 2), to, r * windows : (r + 1) * windows] = wide

    def whiten_own(q):
        @pl.loop(0, rows // WHITEN_ROWS)
        def _(i):
            whiten(q, own, i, WHITEN_ROWS, 0, True)

        send_beside(q).start()

    def expand(q):
        @pl.loop(0, rows // 16)
        def _(i):
            at = pl.ds(pl.multiple_of(i * 16, 16), 16)
            to = pl.ds(pl.multiple_of(rows + i * 16, 16), 16)
            wide = beside[q, at].astype(jnp.float32)
            white[lax.rem(q, 2), to] = wide.reshape(16, 2 * windows, 8, LANES)

    def correlate(group, q, tile, after=None):
        table_a, table_b = tables[2 * group], tables[2 * group + 1]
        source = white.at[lax.rem(q, 2)]
        for t in range(pairs // tile):
            @pl.loop(0, tile // UNROLL)
            def _(i, t=t):
                at = pl.multiple_of(i * UNROLL * 8, 64)
                for u in range(UNROLL):
                    p = t * tile + i * UNROLL + u
                    a, b = source.at[table_a[0, p]], source.at[table_b[0, p]]
                    cross_re, cross_im = None, None
                    for w in range(windows):
                        ar, ai, br, bi = a[w], a[windows + w], b[w], b[windows + w]
                        part_re, part_im = ar * br + ai * bi, ai * br - ar * bi
                        cross_re = part_re if cross_re is None else cross_re + part_re
                        cross_im = part_im if cross_im is None else cross_im + part_im
                    to = pl.ds(at + (u // 8) * 64 + u % 8, 8, stride=8)
                    planes[0, to, :] = cross_re
                    planes[1, to, :] = cross_im

            total = None
            for r in range(2):
                plane = planes[r, 0 : tile * 8].reshape(tile // 8, 8, 8, LANES)
                cross = [plane[:, f].reshape(tile, LANES).astype(jnp.bfloat16) for f in range(8)]
                part = jnp.dot(jnp.concatenate(cross, axis=1), lag[q, r], preferred_element_type=jnp.float32)
                total = part if total is None else total + part
            if after is None:
                acc[group, t * tile : (t + 1) * tile] += total
            else:
                after(t, acc[group, t * tile : (t + 1) * tile] + total)

    def give_back(t, total):
        tile = pairs // RETURNS
        back_out[t * tile : (t + 1) * tile] = total.astype(jnp.bfloat16)
        send_back(t, right).start()

    whiten_own(0)

    @pl.loop(0, slabs)
    def _(q):
        @pl.when(q < slabs - 1)
        def _():
            whiten_own(q + 1)

        send_beside(q).wait_recv()
        expand(q)

        @pl.when(gets)
        def _():
            @pl.loop(0, PIECES)
            def _(k):
                send_across(q, k, right).wait_recv()
                whiten(q, across, k, piece, 2 * rows, False)

            @pl.when(q < slabs - 1)
            def _():
                correlate(1, q, pairs)

            @pl.when(q == slabs - 1)
            def _():
                correlate(1, q, pairs // RETURNS, give_back)

        correlate(0, q, pairs)

    acc[0] = acc[0] * norm_factor
    store = pltpu.make_async_copy(acc.at[0], out_hbm, out_sem.at[0])
    store.start()

    @pl.when(gives)
    def _():
        for t in range(RETURNS):
            send_back(t, left).wait_recv()

    store.wait()
    for q in range(slabs):
        send_beside(q).wait_send()

    @pl.when(core == 0)
    def _():
        hand_over().wait_send()

    @pl.when(core == 1)
    def _():
        for r in range(rounds - 1):
            hop(r).wait_send()
        hand_back().wait_send()

    @pl.when(gives)
    def _():
        for copy in send_tables(left):
            copy.wait_send()

        @pl.loop(0, slabs)
        def _(q):
            for k in range(PIECES):
                send_across(q, k, left).wait_send()

    @pl.when(gets)
    def _():
        for t in range(RETURNS):
            send_back(t, right).wait_send()


def body(spectra, pair_channels, pair_live):
    rows, windows, _, bins = spectra.shape
    count = lax.axis_size("row")
    slabs = bins // SLAB
    view = spectra.reshape(rows, windows, 2, bins // LANES, LANES).transpose(0, 1, 3, 2, 4)
    view = view.reshape(rows, windows, slabs, 16, LANES)
    tile_count, tile_pairs = pair_live.shape
    pairs = tile_count * tile_pairs
    index = jnp.transpose(pair_channels, (2, 0, 1)).reshape(2, pairs)
    live = pair_live.reshape(1, pairs)
    rounds = count.bit_length() - 1
    span = windows * 16
    dma = pltpu.SemaphoreType.DMA
    f32, bf16, i32 = jnp.float32, jnp.bfloat16, jnp.int32
    raw = pltpu.VMEM((slabs, rows, windows, 16, LANES), bf16)
    norm_factor = 1.0 / math.sqrt(bins * windows)
    result, back = pl.pallas_call(
        functools.partial(kernel, count, windows, norm_factor),
        out_shape=[jax.ShapeDtypeStruct((pairs, LAGS), f32), jax.ShapeDtypeStruct((pairs, LAGS), bf16)],
        in_specs=[pl.BlockSpec(memory_space=pltpu.HBM)] * 3,
        out_specs=[pl.BlockSpec(memory_space=pl.ANY)] * 2,
        scratch_shapes=[
            raw,
            pltpu.VMEM((slabs, rows, 2, windows * 8, LANES), bf16),
            pltpu.VMEM((slabs, rows, 2, windows * 8, LANES), bf16),
            raw,
            pltpu.VMEM((2, 3 * rows + 8, 2 * windows, 8, LANES), f32),
            pltpu.VMEM((WHITEN_ROWS * span, LANES), f32),
            pltpu.VMEM((2, pairs * 8, LANES), f32),
            pltpu.VMEM((slabs, 2, SLAB, LAGS), bf16),
            pltpu.VMEM((2, pairs, LAGS), f32),
            pltpu.VMEM((2, LANES, LAGS), f32),
            pltpu.VMEM((2, bins // LANES, LAGS), f32),
            pltpu.VMEM((slabs * span, LANES), f32),
            pltpu.VMEM((slabs * span, LANES), f32),
            pltpu.VMEM((rounds, slabs * span, LANES), f32),
            pltpu.VMEM((rounds - 1, slabs * span, LANES), f32),
            pltpu.VMEM((2, slabs, windows * 8, LANES), f32),
            pltpu.VMEM((2, pairs), i32),
            pltpu.VMEM((1, pairs), i32),
            pltpu.VMEM((2, pairs), i32),
            pltpu.VMEM((1, pairs), i32),
            pltpu.VMEM((4, 1, pairs), i32),
            pltpu.SMEM((1, pairs), i32), pltpu.SMEM((1, pairs), i32),
            pltpu.SMEM((1, pairs), i32), pltpu.SMEM((1, pairs), i32),
            pltpu.VMEM((pairs, LAGS), bf16),
            dma((slabs,)), dma((slabs,)), dma((slabs,)), dma((slabs, PIECES)), dma((slabs, PIECES)),
            dma((rounds + 1,)), dma((rounds + 1,)), dma((2,)), dma((2,)), dma((2,)), dma((RETURNS,)), dma((RETURNS,)), dma((4,)), dma((1,)),
        ],
        compiler_params=pltpu.CompilerParams(
            collective_id=0, has_side_effects=True, vmem_limit_bytes=50 * 2**20),
    )(view, *(pltpu.with_memory_space_constraint(table, pltpu.HBM) for table in (index, live)))
    me = lax.axis_index("row")
    gives = (me & 1) < jnp.minimum(me, 1)
    result = result + jnp.where(gives, back.astype(f32) * norm_factor, 0.0)
    return result.reshape(tile_count, tile_pairs, LAGS)


def solution(mesh):
    placed = (P(("day", "row"), None, None, None), P("row", None, None), P("row", None))
    return jax.shard_map(
        body, mesh=mesh, in_specs=placed, out_specs=P(("day", "row"), None, None), check_vma=False
    )
```

```python
import functools
import math

import jax
import jax.numpy as jnp
from jax import lax
from jax.experimental import pallas as pl
from jax.experimental.pallas import tpu as pltpu
from jax.sharding import PartitionSpec as P

BAND = 64
LAGS = 512
LANES = 128
SLAB = 8 * LANES
PIECES = 2
LAST_PIECES = 2
WHITEN_ROWS = 64
UNROLL = 16
RETURNS = 2
MESH = pl.DeviceIdType.MESH


def kernel(count, windows, norm_factor, own_hbm, pairs_hbm, live_hbm, out_hbm, back_in,
           own, shared, beside, across, across_last, white, spread, planes, lag, acc, base, turn,
           sums, handed, red, heard, common,
           near_pairs, near_live, far_pairs, far_live, tab_v, tab_a0, tab_b0, tab_a1, tab_b1, back_out,
           load_sem, beside_send, beside_recv, across_send, across_recv, last_send, last_recv, sum_send, sum_recv,
           tab_load, tab_send, tab_recv, back_send, back_recv, smem_sem, out_sem):
    slabs, rows = own.shape[:2]
    span = windows * 16
    bins = slabs * SLAB
    pairs = out_hbm.shape[0]
    me = lax.axis_index("row")
    core = lax.rem(me, 2)
    partner = me + 1 - 2 * core
    rounds = count.bit_length() - 1
    last = slabs - 1
    channels = count * rows
    piece = rows // PIECES
    gets = (core == 1) & (me < count - 1)
    gives = (core == 0) & (me > 0)
    right, left = lax.rem(me + 1, count), lax.rem(me + count - 1, count)
    near = jnp.where(core == 1, right, left)
    zero_row = 3 * rows

    def remote(src, dst, sent, got, target):
        return pltpu.make_async_remote_copy(
            src_ref=src, dst_ref=dst, send_sem=sent, recv_sem=got,
            device_id={"row": target}, device_id_type=MESH)

    def load(q):
        return pltpu.make_async_copy(own_hbm.at[:, :, q], own.at[q], load_sem.at[q])

    def send_beside(q):
        return remote(shared.at[q], beside.at[q], beside_send.at[q], beside_recv.at[q], partner)

    def send_across(q, k, target):
        at = pl.ds(pl.multiple_of(k * piece, piece), piece)
        return remote(own_hbm.at[at, :, q], across.at[q, at], across_send.at[q, k], across_recv.at[q, k], target)

    def send_last(w, k, target):
        size = rows // LAST_PIECES
        at = pl.ds(k * size, size)
        return remote(shared.at[last, w, at], across_last.at[w, at],
                      last_send.at[w, k], last_recv.at[w, k], target)

    def send_tables(target):
        return (remote(pairs_hbm, far_pairs, tab_send.at[0], tab_recv.at[0], target),
                remote(live_hbm, far_live, tab_send.at[1], tab_recv.at[1], target))

    fetches = (pltpu.make_async_copy(pairs_hbm, near_pairs, tab_load.at[0]),
               pltpu.make_async_copy(live_hbm, near_live, tab_load.at[1]))

    def send_back(t, target):
        at = pl.ds(t * (pairs // RETURNS), pairs // RETURNS)
        return remote(back_out.at[at], back_in.at[at], back_send.at[t], back_recv.at[t], target)

    for q in range(slabs):
        load(q).start()
    for fetch in fetches:
        fetch.start()

    barrier = pltpu.get_barrier_semaphore()
    hops = [me ^ (1 << r) for r in range(1, rounds)]
    for p in (partner, near):
        pl.semaphore_signal(barrier, inc=1, device_id={"row": p}, device_id_type=MESH)

    @pl.when(core == 1)
    def _():
        for p in hops:
            pl.semaphore_signal(barrier, inc=1, device_id={"row": p}, device_id_type=MESH)

    pl.semaphore_wait(barrier, 2 + core * len(hops))

    @pl.when(gives)
    def _():
        for copy in send_tables(left):
            copy.start()

        @pl.loop(0, last)
        def _(q):
            for k in range(PIECES):
                send_across(q, k, left).start()

    acc[...] = jnp.zeros_like(acc)
    for h in range(2):
        white[h, pl.ds(zero_row, 8)] = jnp.zeros((8,) + white.shape[2:], jnp.float32)

    for q in range(slabs):
        load(q).wait()

        def step(i, total):
            block = own[q, pl.ds(pl.multiple_of(i * 8, 8), 8)].astype(jnp.float32)
            return total + jnp.sum(block, axis=0)

        total = lax.fori_loop(0, rows // 8, step, jnp.zeros((windows, 16, LANES), jnp.float32))
        sums[pl.ds(q * span, span), :] = total.reshape(span, LANES)

    def hand_over():
        return remote(sums, handed, sum_send.at[0], sum_recv.at[0], partner)

    def hop(r):
        return remote(red.at[r], heard.at[r], sum_send.at[r + 1], sum_recv.at[r + 1], hops[r])

    def hand_back():
        return remote(red.at[rounds - 1], handed, sum_send.at[rounds], sum_recv.at[rounds], partner)

    @pl.when(core == 0)
    def _():
        hand_over().start()

    shifts = lax.broadcasted_iota(jnp.int32, (LANES, LAGS), 1) + (2 * bins - LAGS // 2)
    phase = lax.rem(lax.broadcasted_iota(jnp.int32, (LANES, LAGS), 0) * shifts, 2 * bins)
    angle = phase.astype(jnp.float32) * (math.pi / bins)
    base[0] = jnp.cos(angle)
    base[1] = jnp.sin(angle)

    @pl.when(core == 1)
    def _():
        hand_over().wait_recv()
        red[0] = sums[...] + handed[...]
        hop(0).start()

    tiles = bins // LANES
    shift_row = lax.broadcasted_iota(jnp.int32, (tiles, LAGS), 1) + (2 * bins - LAGS // 2)
    turns = lax.rem(lax.broadcasted_iota(jnp.int32, (tiles, LAGS), 0) * shift_row, 2 * bins)
    turned = lax.rem(turns * LANES, 2 * bins).astype(jnp.float32) * (math.pi / bins)
    turn[0] = jnp.cos(turned)
    turn[1] = jnp.sin(turned)

    for r in range(rounds - 1):
        @pl.loop(r * slabs // (rounds - 1), (r + 1) * slabs // (rounds - 1))
        def _(q):
            @pl.loop(0, 8)
            def _(f):
                ch = turn[0, pl.ds(q * 8 + f, 1), :]
                sh = turn[1, pl.ds(q * 8 + f, 1), :]

                @pl.loop(0, LANES // 16)
                def _(k):
                    at = pl.ds(pl.multiple_of(k * 16, 16), 16)
                    to = pl.ds(pl.multiple_of(f * LANES + k * 16, 16), 16)
                    bc, bs = base[0, at, :], base[1, at, :]
                    lag[q, 0, to, :] = (bc * ch - bs * sh).astype(jnp.bfloat16)
                    lag[q, 1, to, :] = (-(bs * ch + bc * sh)).astype(jnp.bfloat16)

        @pl.when(core == 1)
        def _():
            hop(r).wait_recv()
            red[r + 1] = red[r] + heard[r]
            if r + 2 < rounds:
                hop(r + 1).start()
            else:
                hand_back().start()

    def place(index, regions):
        slot = jnp.full_like(index, zero_row)
        for device, start in regions:
            offset = index - device * rows
            slot = jnp.where((offset >= 0) & (offset < rows), offset + start, slot)
        return slot

    for fetch in fetches:
        fetch.wait()
    first, second, live = near_pairs[0:1], near_pairs[1:2], near_live[...]
    far_device = jnp.where(gets, me + 1, -2)
    regions = ((me, 0), (partner, rows), (far_device, 2 * rows))
    tab_v[0] = jnp.where(live > 0, place(first, regions), zero_row)
    tab_v[1] = place(second, regions)

    @pl.when(gets)
    def _():
        for copy in send_tables(right):
            copy.wait_recv()
        tab_v[2] = jnp.where(far_live[...] > 0, place(far_pairs[0:1], ((me + 1, 2 * rows),)), zero_row)
        tab_v[3] = place(far_pairs[1:2], ((me, 0),))

    @pl.when(jnp.logical_not(gets))
    def _():
        tab_v[2] = jnp.full((1, pairs), zero_row, jnp.int32)
        tab_v[3] = jnp.full((1, pairs), zero_row, jnp.int32)

    tables = (tab_a0, tab_b0, tab_a1, tab_b1)
    moves = [pltpu.make_async_copy(tab_v.at[i], table, smem_sem.at[i]) for i, table in enumerate(tables)]
    for move in moves:
        move.start()

    def set_common(total):
        for r in range(2):
            strided = total[pl.ds(r, slabs * windows * 8, stride=2), :] * (1.0 / channels)
            common[r] = strided.reshape(slabs, windows * 8, LANES)

    @pl.when(core == 1)
    def _():
        set_common(red.at[rounds - 1])

    @pl.when(core == 0)
    def _():
        hand_back().wait_recv()
        set_common(handed)

    for move in moves:
        move.wait()

    lane_r = lax.broadcasted_iota(jnp.int32, (LANES, LANES), 0) // BAND
    lane_c = lax.broadcasted_iota(jnp.int32, (LANES, LANES), 1) // BAND
    same = (lane_r == lane_c).astype(jnp.float32).astype(jnp.bfloat16)
    depth = windows * 8

    def whiten(q, source, i, size, start, keep):
        at = pl.ds(pl.multiple_of(i * size, size), size)
        spread[0 : size * span] = source[q, at].astype(jnp.float32).reshape(size * span, LANES)
        re = spread[pl.ds(0, size * depth, stride=2), :].reshape(size, depth, LANES) - common[0, q][None]
        im = spread[pl.ds(1, size * depth, stride=2), :].reshape(size, depth, LANES) - common[1, q][None]
        power = (re * re + im * im).reshape(size * depth, LANES)
        mag = power * lax.rsqrt(jnp.maximum(power, 1e-30))
        hi = mag.astype(jnp.bfloat16)
        lo = (mag - hi.astype(jnp.float32)).astype(jnp.bfloat16)
        level = jnp.dot(hi, same, preferred_element_type=jnp.float32)
        level += jnp.dot(lo, same, preferred_element_type=jnp.float32)
        scale = (1.0 / (level * (1.0 / BAND) + 1e-06)).reshape(size, depth, LANES)
        to = pl.ds(pl.multiple_of(start + i * size, 8), size)
        for r, part in enumerate((re, im)):
            rounded = (part * scale).astype(jnp.bfloat16)
            if keep:
                for w in range(windows):
                    shared[q, w, at, r] = rounded[:, w * 8 : (w + 1) * 8]
            wide = rounded.astype(jnp.float32).reshape(size, windows, 8, LANES)
            white[lax.rem(q, 2), to, r * windows : (r + 1) * windows] = wide

    def whiten_own(q):
        @pl.loop(0, rows // WHITEN_ROWS)
        def _(i):
            whiten(q, own, i, WHITEN_ROWS, 0, True)

        send_beside(q).start()

    def expand(q):
        @pl.loop(0, rows // 16)
        def _(i):
            at = pl.ds(pl.multiple_of(i * 16, 16), 16)
            to = pl.ds(pl.multiple_of(rows + i * 16, 16), 16)
            for w in range(windows):
                wide = beside[q, w, at].astype(jnp.float32)
                white[lax.rem(q, 2), to, w] = wide[:, 0]
                white[lax.rem(q, 2), to, windows + w] = wide[:, 1]

    def expand_last(w, k):
        size = rows // LAST_PIECES
        wide = across_last[w, k * size : (k + 1) * size].astype(jnp.float32)
        to = slice(2 * rows + k * size, 2 * rows + (k + 1) * size)
        white[last % 2, to, w] = wide[:, 0]
        white[last % 2, to, windows + w] = wide[:, 1]

    def correlate(group, q, tile, after=None, used=tuple(range(windows))):
        table_a, table_b = tables[2 * group], tables[2 * group + 1]
        source = white.at[lax.rem(q, 2)]
        for t in range(pairs // tile):
            @pl.loop(0, tile // UNROLL)
            def _(i, t=t):
                at = pl.multiple_of(i * UNROLL * 8, 64)
                for u in range(UNROLL):
                    p = t * tile + i * UNROLL + u
                    a, b = source.at[table_a[0, p]], source.at[table_b[0, p]]
                    cross_re, cross_im = None, None
                    for w in used:
                        ar, ai, br, bi = a[w], a[windows + w], b[w], b[windows + w]
                        part_re, part_im = ar * br + ai * bi, ai * br - ar * bi
                        cross_re = part_re if cross_re is None else cross_re + part_re
                        cross_im = part_im if cross_im is None else cross_im + part_im
                    to = pl.ds(at + (u // 8) * 64 + u % 8, 8, stride=8)
                    planes[0, to, :] = cross_re
                    planes[1, to, :] = cross_im

            total = None
            for r in range(2):
                plane = planes[r, 0 : tile * 8].reshape(tile // 8, 8, 8, LANES)
                cross = [plane[:, f].reshape(tile, LANES).astype(jnp.bfloat16) for f in range(8)]
                part = jnp.dot(jnp.concatenate(cross, axis=1), lag[q, r], preferred_element_type=jnp.float32)
                total = part if total is None else total + part
            if after is None:
                acc[group, t * tile : (t + 1) * tile] += total
            else:
                after(t, acc[group, t * tile : (t + 1) * tile] + total)

    def give_back(t, total):
        tile = pairs // RETURNS
        back_out[t * tile : (t + 1) * tile] = total.astype(jnp.bfloat16)
        send_back(t, right).start()

    whiten_own(0)

    @pl.loop(0, slabs)
    def _(q):
        @pl.when(q < slabs - 1)
        def _():
            whiten_own(q + 1)

        @pl.when(gives & (q == last - 1))
        def _():
            for w in range(windows):
                for k in range(LAST_PIECES):
                    send_last(w, k, left).start()

        send_beside(q).wait_recv()
        expand(q)

        @pl.when(gets)
        def _():
            @pl.when(q < last)
            def _():
                @pl.loop(0, PIECES)
                def _(k):
                    send_across(q, k, right).wait_recv()
                    whiten(q, across, k, piece, 2 * rows, False)

                correlate(1, q, pairs)

            @pl.when(q == last)
            def _():
                for w in range(windows):
                    for k in range(LAST_PIECES):
                        send_last(w, k, right).wait_recv()
                        expand_last(w, k)
                    if w < windows - 1:
                        correlate(1, q, pairs, None, (w,))
                    else:
                        correlate(1, q, pairs // RETURNS, give_back, (w,))

        correlate(0, q, pairs)

    acc[0] = acc[0] * norm_factor
    store = pltpu.make_async_copy(acc.at[0], out_hbm, out_sem.at[0])
    store.start()

    @pl.when(gives)
    def _():
        for t in range(RETURNS):
            send_back(t, left).wait_recv()

    store.wait()
    for q in range(slabs):
        send_beside(q).wait_send()

    @pl.when(core == 0)
    def _():
        hand_over().wait_send()

    @pl.when(core == 1)
    def _():
        for r in range(rounds - 1):
            hop(r).wait_send()
        hand_back().wait_send()

    @pl.when(gives)
    def _():
        for copy in send_tables(left):
            copy.wait_send()

        @pl.loop(0, last)
        def _(q):
            for k in range(PIECES):
                send_across(q, k, left).wait_send()
        for w in range(windows):
            for k in range(LAST_PIECES):
                send_last(w, k, left).wait_send()

    @pl.when(gets)
    def _():
        for t in range(RETURNS):
            send_back(t, right).wait_send()


def body(spectra, pair_channels, pair_live):
    rows, windows, _, bins = spectra.shape
    count = lax.axis_size("row")
    slabs = bins // SLAB
    view = spectra.reshape(rows, windows, 2, bins // LANES, LANES).transpose(0, 1, 3, 2, 4)
    view = view.reshape(rows, windows, slabs, 16, LANES)
    tile_count, tile_pairs = pair_live.shape
    pairs = tile_count * tile_pairs
    index = jnp.transpose(pair_channels, (2, 0, 1)).reshape(2, pairs)
    live = pair_live.reshape(1, pairs)
    rounds = count.bit_length() - 1
    span = windows * 16
    dma = pltpu.SemaphoreType.DMA
    f32, bf16, i32 = jnp.float32, jnp.bfloat16, jnp.int32
    raw = pltpu.VMEM((slabs, rows, windows, 16, LANES), bf16)
    norm_factor = 1.0 / math.sqrt(bins * windows)
    result, back = pl.pallas_call(
        functools.partial(kernel, count, windows, norm_factor),
        out_shape=[jax.ShapeDtypeStruct((pairs, LAGS), f32), jax.ShapeDtypeStruct((pairs, LAGS), bf16)],
        in_specs=[pl.BlockSpec(memory_space=pltpu.HBM)] * 3,
        out_specs=[pl.BlockSpec(memory_space=pl.ANY)] * 2,
        scratch_shapes=[
            raw,
            pltpu.VMEM((slabs, windows, rows, 2, 8, LANES), bf16),
            pltpu.VMEM((slabs, windows, rows, 2, 8, LANES), bf16),
            pltpu.VMEM((slabs - 1, rows, windows, 16, LANES), bf16),
            pltpu.VMEM((windows, rows, 2, 8, LANES), bf16),
            pltpu.VMEM((2, 3 * rows + 8, 2 * windows, 8, LANES), f32),
            pltpu.VMEM((WHITEN_ROWS * span, LANES), f32),
            pltpu.VMEM((2, pairs * 8, LANES), f32),
            pltpu.VMEM((slabs, 2, SLAB, LAGS), bf16),
            pltpu.VMEM((2, pairs, LAGS), f32),
            pltpu.VMEM((2, LANES, LAGS), f32),
            pltpu.VMEM((2, bins // LANES, LAGS), f32),
            pltpu.VMEM((slabs * span, LANES), f32),
            pltpu.VMEM((slabs * span, LANES), f32),
            pltpu.VMEM((rounds, slabs * span, LANES), f32),
            pltpu.VMEM((rounds - 1, slabs * span, LANES), f32),
            pltpu.VMEM((2, slabs, windows * 8, LANES), f32),
            pltpu.VMEM((2, pairs), i32),
            pltpu.VMEM((1, pairs), i32),
            pltpu.VMEM((2, pairs), i32),
            pltpu.VMEM((1, pairs), i32),
            pltpu.VMEM((4, 1, pairs), i32),
            pltpu.SMEM((1, pairs), i32), pltpu.SMEM((1, pairs), i32),
            pltpu.SMEM((1, pairs), i32), pltpu.SMEM((1, pairs), i32),
            pltpu.VMEM((pairs, LAGS), bf16),
            dma((slabs,)), dma((slabs,)), dma((slabs,)), dma((slabs - 1, PIECES)), dma((slabs - 1, PIECES)),
            dma((windows, LAST_PIECES)), dma((windows, LAST_PIECES)),
            dma((rounds + 1,)), dma((rounds + 1,)), dma((2,)), dma((2,)), dma((2,)), dma((RETURNS,)), dma((RETURNS,)), dma((4,)), dma((1,)),
        ],
        compiler_params=pltpu.CompilerParams(
            collective_id=0, has_side_effects=True, vmem_limit_bytes=50 * 2**20),
    )(view, *(pltpu.with_memory_space_constraint(table, pltpu.HBM) for table in (index, live)))
    me = lax.axis_index("row")
    gives = (me & 1) < jnp.minimum(me, 1)
    result = result + jnp.where(gives, back.astype(f32) * norm_factor, 0.0)
    return result.reshape(tile_count, tile_pairs, LAGS)


def solution(mesh):
    placed = (P(("day", "row"), None, None, None), P("row", None, None), P("row", None))
    return jax.shard_map(
        body, mesh=mesh, in_specs=placed, out_specs=P(("day", "row"), None, None), check_vma=False
    )
```

```python
import functools
import math

import jax
import jax.numpy as jnp
from jax import lax
from jax.experimental import pallas as pl
from jax.experimental.pallas import tpu as pltpu
from jax.sharding import PartitionSpec as P

BAND = 64
LAGS = 512
LANES = 128
SLAB = 8 * LANES
PIECES = 2
LAST_PIECES = 2
WHITEN_ROWS = 64
UNROLL = 32
RETURNS = 2
MESH = pl.DeviceIdType.MESH


def kernel(count, windows, norm_factor, own_hbm, pairs_hbm, live_hbm, out_ref,
           own, shared, beside, across, across_last, white, spread, planes, lag, acc, base, turn,
           sums, handed, red, heard, common,
           near_pairs, near_live, far_pairs, far_live, tab_v, tab_a0, tab_b0, tab_a1, tab_b1, back,
           load_sem, beside_send, beside_recv, across_send, across_recv, last_send, last_recv, sum_send, sum_recv,
           tab_load, tab_send, tab_recv, back_send, back_recv, smem_sem):
    slabs, rows = own.shape[:2]
    span = windows * 16
    bins = slabs * SLAB
    pairs = out_ref.shape[0]
    me = lax.axis_index("row")
    core = lax.rem(me, 2)
    partner = me + 1 - 2 * core
    rounds = count.bit_length() - 1
    last = slabs - 1
    channels = count * rows
    piece = rows // PIECES
    gets = (core == 1) & (me < count - 1)
    gives = (core == 0) & (me > 0)
    right, left = lax.rem(me + 1, count), lax.rem(me + count - 1, count)
    near = jnp.where(core == 1, right, left)
    zero_row = 3 * rows

    def remote(src, dst, sent, got, target):
        return pltpu.make_async_remote_copy(
            src_ref=src, dst_ref=dst, send_sem=sent, recv_sem=got,
            device_id={"row": target}, device_id_type=MESH)

    def load(q):
        return pltpu.make_async_copy(own_hbm.at[:, :, q], own.at[q], load_sem.at[q])

    def send_beside(q):
        return remote(shared.at[q], beside.at[q], beside_send.at[q], beside_recv.at[q], partner)

    def send_across(q, k, target):
        at = pl.ds(pl.multiple_of(k * piece, piece), piece)
        return remote(own_hbm.at[at, :, q], across.at[q, at], across_send.at[q, k], across_recv.at[q, k], target)

    def send_last(w, k, target):
        size = rows // LAST_PIECES
        at = pl.ds(k * size, size)
        return remote(shared.at[last, w, at], across_last.at[w, at],
                      last_send.at[w, k], last_recv.at[w, k], target)

    def send_tables(target):
        return (remote(pairs_hbm, far_pairs, tab_send.at[0], tab_recv.at[0], target),
                remote(live_hbm, far_live, tab_send.at[1], tab_recv.at[1], target))

    fetches = (pltpu.make_async_copy(pairs_hbm, near_pairs, tab_load.at[0]),
               pltpu.make_async_copy(live_hbm, near_live, tab_load.at[1]))

    def send_back(t, target):
        at = pl.ds(t * (pairs // RETURNS), pairs // RETURNS)
        return remote(back.at[at], back.at[at], back_send.at[t], back_recv.at[t], target)

    for q in range(slabs):
        load(q).start()
    for fetch in fetches:
        fetch.start()

    barrier = pltpu.get_barrier_semaphore()
    hops = [me ^ (1 << r) for r in range(1, rounds)]
    for p in (partner, near):
        pl.semaphore_signal(barrier, inc=1, device_id={"row": p}, device_id_type=MESH)

    @pl.when(core == 1)
    def _():
        for p in hops:
            pl.semaphore_signal(barrier, inc=1, device_id={"row": p}, device_id_type=MESH)

    pl.semaphore_wait(barrier, 2 + core * len(hops))

    @pl.when(gives)
    def _():
        for copy in send_tables(left):
            copy.start()

        @pl.loop(0, last)
        def _(q):
            for k in range(PIECES):
                send_across(q, k, left).start()

    acc[...] = jnp.zeros_like(acc)
    for h in range(2):
        white[h, pl.ds(zero_row, 8)] = jnp.zeros((8,) + white.shape[2:], jnp.float32)

    for q in range(slabs):
        load(q).wait()

        def step(i, total):
            block = own[q, pl.ds(pl.multiple_of(i * 8, 8), 8)].astype(jnp.float32)
            return total + jnp.sum(block, axis=0)

        total = lax.fori_loop(0, rows // 8, step, jnp.zeros((windows, 16, LANES), jnp.float32))
        sums[pl.ds(q * span, span), :] = total.reshape(span, LANES)

    def hand_over():
        return remote(sums, handed, sum_send.at[0], sum_recv.at[0], partner)

    def hop(r):
        return remote(red.at[r], heard.at[r], sum_send.at[r + 1], sum_recv.at[r + 1], hops[r])

    def hand_back():
        return remote(red.at[rounds - 1], handed, sum_send.at[rounds], sum_recv.at[rounds], partner)

    @pl.when(core == 0)
    def _():
        hand_over().start()

    shifts = lax.broadcasted_iota(jnp.int32, (LANES, LAGS), 1) + (2 * bins - LAGS // 2)
    phase = lax.rem(lax.broadcasted_iota(jnp.int32, (LANES, LAGS), 0) * shifts, 2 * bins)
    angle = phase.astype(jnp.float32) * (math.pi / bins)
    base[0] = jnp.cos(angle)
    base[1] = jnp.sin(angle)

    @pl.when(core == 1)
    def _():
        hand_over().wait_recv()
        red[0] = sums[...] + handed[...]
        hop(0).start()

    tiles = bins // LANES
    shift_row = lax.broadcasted_iota(jnp.int32, (tiles, LAGS), 1) + (2 * bins - LAGS // 2)
    turns = lax.rem(lax.broadcasted_iota(jnp.int32, (tiles, LAGS), 0) * shift_row, 2 * bins)
    turned = lax.rem(turns * LANES, 2 * bins).astype(jnp.float32) * (math.pi / bins)
    turn[0] = jnp.cos(turned)
    turn[1] = jnp.sin(turned)

    for r in range(rounds - 1):
        @pl.loop(r * slabs // (rounds - 1), (r + 1) * slabs // (rounds - 1))
        def _(q):
            @pl.loop(0, 8)
            def _(f):
                ch = turn[0, pl.ds(q * 8 + f, 1), :]
                sh = turn[1, pl.ds(q * 8 + f, 1), :]

                @pl.loop(0, LANES // 16)
                def _(k):
                    at = pl.ds(pl.multiple_of(k * 16, 16), 16)
                    to = pl.ds(pl.multiple_of(f * LANES + k * 16, 16), 16)
                    bc, bs = base[0, at, :], base[1, at, :]
                    lag[q, 0, to, :] = (bc * ch - bs * sh).astype(jnp.bfloat16)
                    lag[q, 1, to, :] = (-(bs * ch + bc * sh)).astype(jnp.bfloat16)

        @pl.when(core == 1)
        def _():
            hop(r).wait_recv()
            red[r + 1] = red[r] + heard[r]
            if r + 2 < rounds:
                hop(r + 1).start()
            else:
                hand_back().start()

    def place(index, regions):
        slot = jnp.full_like(index, zero_row)
        for device, start in regions:
            offset = index - device * rows
            slot = jnp.where((offset >= 0) & (offset < rows), offset + start, slot)
        return slot

    for fetch in fetches:
        fetch.wait()
    first, second, live = near_pairs[0:1], near_pairs[1:2], near_live[...]
    far_device = jnp.where(gets, me + 1, -2)
    regions = ((me, 0), (partner, rows), (far_device, 2 * rows))
    tab_v[0] = jnp.where(live > 0, place(first, regions), zero_row)
    tab_v[1] = place(second, regions)

    @pl.when(gets)
    def _():
        for copy in send_tables(right):
            copy.wait_recv()
        tab_v[2] = jnp.where(far_live[...] > 0, place(far_pairs[0:1], ((me + 1, 2 * rows),)), zero_row)
        tab_v[3] = place(far_pairs[1:2], ((me, 0),))

    @pl.when(jnp.logical_not(gets))
    def _():
        tab_v[2] = jnp.full((1, pairs), zero_row, jnp.int32)
        tab_v[3] = jnp.full((1, pairs), zero_row, jnp.int32)

    tables = (tab_a0, tab_b0, tab_a1, tab_b1)
    moves = [pltpu.make_async_copy(tab_v.at[i], table, smem_sem.at[i]) for i, table in enumerate(tables)]
    for move in moves:
        move.start()

    def set_common(total):
        for r in range(2):
            strided = total[pl.ds(r, slabs * windows * 8, stride=2), :] * (1.0 / channels)
            common[r] = strided.reshape(slabs, windows * 8, LANES)

    @pl.when(core == 1)
    def _():
        set_common(red.at[rounds - 1])

    @pl.when(core == 0)
    def _():
        hand_back().wait_recv()
        set_common(handed)

    for move in moves:
        move.wait()

    lane_r = lax.broadcasted_iota(jnp.int32, (LANES, LANES), 0) // BAND
    lane_c = lax.broadcasted_iota(jnp.int32, (LANES, LANES), 1) // BAND
    same = (lane_r == lane_c).astype(jnp.float32).astype(jnp.bfloat16)
    depth = windows * 8

    def whiten(q, source, i, size, start, keep):
        at = pl.ds(pl.multiple_of(i * size, size), size)
        spread[0 : size * span] = source[q, at].astype(jnp.float32).reshape(size * span, LANES)
        re = spread[pl.ds(0, size * depth, stride=2), :].reshape(size, depth, LANES) - common[0, q][None]
        im = spread[pl.ds(1, size * depth, stride=2), :].reshape(size, depth, LANES) - common[1, q][None]
        power = (re * re + im * im).reshape(size * depth, LANES)
        mag = power * lax.rsqrt(jnp.maximum(power, 1e-30))
        hi = mag.astype(jnp.bfloat16)
        lo = (mag - hi.astype(jnp.float32)).astype(jnp.bfloat16)
        level = jnp.dot(hi, same, preferred_element_type=jnp.float32)
        level += jnp.dot(lo, same, preferred_element_type=jnp.float32)
        scale = (1.0 / (level * (1.0 / BAND) + 1e-06)).reshape(size, depth, LANES)
        to = pl.ds(pl.multiple_of(start + i * size, 8), size)
        for r, part in enumerate((re, im)):
            rounded = (part * scale).astype(jnp.bfloat16)
            if keep:
                for w in range(windows):
                    shared[q, w, at, r] = rounded[:, w * 8 : (w + 1) * 8]
            wide = rounded.astype(jnp.float32).reshape(size, windows, 8, LANES)
            white[lax.rem(q, 2), to, r * windows : (r + 1) * windows] = wide

    def whiten_own(q):
        @pl.loop(0, rows // WHITEN_ROWS)
        def _(i):
            whiten(q, own, i, WHITEN_ROWS, 0, True)

        send_beside(q).start()

    def expand(q):
        @pl.loop(0, rows // 16)
        def _(i):
            at = pl.ds(pl.multiple_of(i * 16, 16), 16)
            to = pl.ds(pl.multiple_of(rows + i * 16, 16), 16)
            for w in range(windows):
                wide = beside[q, w, at].astype(jnp.float32)
                white[lax.rem(q, 2), to, w] = wide[:, 0]
                white[lax.rem(q, 2), to, windows + w] = wide[:, 1]

    def expand_last(w, k):
        size = rows // LAST_PIECES
        wide = across_last[w, k * size : (k + 1) * size].astype(jnp.float32)
        to = slice(2 * rows + k * size, 2 * rows + (k + 1) * size)
        white[last % 2, to, w] = wide[:, 0]
        white[last % 2, to, windows + w] = wide[:, 1]

    def correlate(group, q, tile, after=None, used=tuple(range(windows))):
        table_a, table_b = tables[2 * group], tables[2 * group + 1]
        source = white.at[lax.rem(q, 2)]
        for t in range(pairs // tile):
            @pl.loop(0, tile // UNROLL)
            def _(i, t=t):
                at = pl.multiple_of(i * UNROLL * 8, 64)
                for u in range(UNROLL):
                    p = t * tile + i * UNROLL + u
                    a, b = source.at[table_a[0, p]], source.at[table_b[0, p]]
                    cross_re, cross_im = None, None
                    for w in used:
                        ar, ai, br, bi = a[w], a[windows + w], b[w], b[windows + w]
                        part_re, part_im = ar * br + ai * bi, ai * br - ar * bi
                        cross_re = part_re if cross_re is None else cross_re + part_re
                        cross_im = part_im if cross_im is None else cross_im + part_im
                    to = pl.ds(at + (u // 8) * 64 + u % 8, 8, stride=8)
                    planes[0, to, :] = cross_re
                    planes[1, to, :] = cross_im

            total = None
            for r in range(2):
                plane = planes[r, 0 : tile * 8].reshape(tile // 8, 8, 8, LANES)
                cross = [plane[:, f].reshape(tile, LANES).astype(jnp.bfloat16) for f in range(8)]
                part = jnp.dot(jnp.concatenate(cross, axis=1), lag[q, r], preferred_element_type=jnp.float32)
                total = part if total is None else total + part
            if after is None:
                acc[group, t * tile : (t + 1) * tile] += total
            else:
                after(t, acc[group, t * tile : (t + 1) * tile] + total)

    def give_back(t, total):
        tile = pairs // RETURNS
        back[t * tile : (t + 1) * tile] = total.astype(jnp.bfloat16)
        send_back(t, right).start()

    whiten_own(0)

    @pl.loop(0, slabs)
    def _(q):
        @pl.when(q < slabs - 1)
        def _():
            whiten_own(q + 1)

        @pl.when(gives & (q == last - 1))
        def _():
            for w in range(windows):
                for k in range(LAST_PIECES):
                    send_last(w, k, left).start()

        send_beside(q).wait_recv()
        expand(q)

        @pl.when(gets)
        def _():
            @pl.when(q < last)
            def _():
                @pl.loop(0, PIECES)
                def _(k):
                    send_across(q, k, right).wait_recv()
                    whiten(q, across, k, piece, 2 * rows, False)

                correlate(1, q, pairs)

            @pl.when(q == last)
            def _():
                for w in range(windows):
                    for k in range(LAST_PIECES):
                        send_last(w, k, right).wait_recv()
                        expand_last(w, k)
                    if w < windows - 1:
                        correlate(1, q, pairs, None, (w,))
                    else:
                        correlate(1, q, pairs // RETURNS, give_back, (w,))

        correlate(0, q, pairs)

    out_ref[...] = acc[0] * norm_factor

    @pl.when(gives)
    def _():
        for t in range(RETURNS):
            send_back(t, left).wait_recv()
            at = pl.ds(t * (pairs // RETURNS), pairs // RETURNS)
            out_ref[at] = out_ref[at] + back[at].astype(jnp.float32) * norm_factor

    for q in range(slabs):
        send_beside(q).wait_send()

    @pl.when(core == 0)
    def _():
        hand_over().wait_send()

    @pl.when(core == 1)
    def _():
        for r in range(rounds - 1):
            hop(r).wait_send()
        hand_back().wait_send()

    @pl.when(gives)
    def _():
        for copy in send_tables(left):
            copy.wait_send()

        @pl.loop(0, last)
        def _(q):
            for k in range(PIECES):
                send_across(q, k, left).wait_send()
        for w in range(windows):
            for k in range(LAST_PIECES):
                send_last(w, k, left).wait_send()

    @pl.when(gets)
    def _():
        for t in range(RETURNS):
            send_back(t, right).wait_send()


def body(spectra, pair_channels, pair_live):
    rows, windows, _, bins = spectra.shape
    count = lax.axis_size("row")
    slabs = bins // SLAB
    view = spectra.reshape(rows, windows, 2, bins // LANES, LANES).transpose(0, 1, 3, 2, 4)
    view = view.reshape(rows, windows, slabs, 16, LANES)
    tile_count, tile_pairs = pair_live.shape
    pairs = tile_count * tile_pairs
    index = jnp.transpose(pair_channels, (2, 0, 1)).reshape(2, pairs)
    live = pair_live.reshape(1, pairs)
    rounds = count.bit_length() - 1
    span = windows * 16
    dma = pltpu.SemaphoreType.DMA
    f32, bf16, i32 = jnp.float32, jnp.bfloat16, jnp.int32
    raw = pltpu.VMEM((slabs, rows, windows, 16, LANES), bf16)
    norm_factor = 1.0 / math.sqrt(bins * windows)
    result = pl.pallas_call(
        functools.partial(kernel, count, windows, norm_factor),
        out_shape=jax.ShapeDtypeStruct((pairs, LAGS), f32),
        in_specs=[pl.BlockSpec(memory_space=pltpu.HBM)] * 3,
        out_specs=pl.BlockSpec(memory_space=pltpu.VMEM),
        scratch_shapes=[
            raw,
            pltpu.VMEM((slabs, windows, rows, 2, 8, LANES), bf16),
            pltpu.VMEM((slabs, windows, rows, 2, 8, LANES), bf16),
            pltpu.VMEM((slabs - 1, rows, windows, 16, LANES), bf16),
            pltpu.VMEM((windows, rows, 2, 8, LANES), bf16),
            pltpu.VMEM((2, 3 * rows + 8, 2 * windows, 8, LANES), f32),
            pltpu.VMEM((WHITEN_ROWS * span, LANES), f32),
            pltpu.VMEM((2, pairs * 8, LANES), f32),
            pltpu.VMEM((slabs, 2, SLAB, LAGS), bf16),
            pltpu.VMEM((2, pairs, LAGS), f32),
            pltpu.VMEM((2, LANES, LAGS), f32),
            pltpu.VMEM((2, bins // LANES, LAGS), f32),
            pltpu.VMEM((slabs * span, LANES), f32),
            pltpu.VMEM((slabs * span, LANES), f32),
            pltpu.VMEM((rounds, slabs * span, LANES), f32),
            pltpu.VMEM((rounds - 1, slabs * span, LANES), f32),
            pltpu.VMEM((2, slabs, windows * 8, LANES), f32),
            pltpu.VMEM((2, pairs), i32),
            pltpu.VMEM((1, pairs), i32),
            pltpu.VMEM((2, pairs), i32),
            pltpu.VMEM((1, pairs), i32),
            pltpu.VMEM((4, 1, pairs), i32),
            pltpu.SMEM((1, pairs), i32), pltpu.SMEM((1, pairs), i32),
            pltpu.SMEM((1, pairs), i32), pltpu.SMEM((1, pairs), i32),
            pltpu.VMEM((pairs, LAGS), bf16),
            dma((slabs,)), dma((slabs,)), dma((slabs,)), dma((slabs - 1, PIECES)), dma((slabs - 1, PIECES)),
            dma((windows, LAST_PIECES)), dma((windows, LAST_PIECES)),
            dma((rounds + 1,)), dma((rounds + 1,)), dma((2,)), dma((2,)), dma((2,)), dma((RETURNS,)), dma((RETURNS,)), dma((4,)),
        ],
        compiler_params=pltpu.CompilerParams(
            collective_id=0, has_side_effects=True, vmem_limit_bytes=50 * 2**20),
    )(view, *(pltpu.with_memory_space_constraint(table, pltpu.HBM) for table in (index, live)))
    return result.reshape(tile_count, tile_pairs, LAGS)


def solution(mesh):
    placed = (P(("day", "row"), None, None, None), P("row", None, None), P("row", None))
    return jax.shard_map(
        body, mesh=mesh, in_specs=placed, out_specs=P(("day", "row"), None, None), check_vma=False
    )
```

```python
import functools
import math

import jax
import jax.numpy as jnp
from jax import lax
from jax.experimental import pallas as pl
from jax.experimental.pallas import tpu as pltpu
from jax.sharding import PartitionSpec as P

BAND = 64
LAGS = 512
LANES = 128
SLAB = 8 * LANES
PIECES = 1
LAST_PIECES = 1
WHITEN_ROWS = 64
UNROLL = 32
RETURNS = 2
MESH = pl.DeviceIdType.MESH


def kernel(count, windows, norm_factor, own_hbm, pairs_hbm, live_hbm, out_ref,
           own, shared, beside, across, across_last, white, spread, planes, lag, acc, base, turn,
           sums, handed, red, heard, common,
           near_pairs, near_live, far_pairs, far_live, tab_v, tab_a0, tab_b0, tab_a1, tab_b1, back,
           load_sem, beside_send, beside_recv, across_send, across_recv, last_send, last_recv, sum_send, sum_recv,
           tab_load, tab_send, tab_recv, back_send, back_recv, smem_sem):
    slabs, rows = own.shape[:2]
    span = windows * 16
    bins = slabs * SLAB
    pairs = out_ref.shape[0]
    me = lax.axis_index("row")
    core = lax.rem(me, 2)
    partner = me + 1 - 2 * core
    rounds = count.bit_length() - 1
    last = slabs - 1
    channels = count * rows
    piece = rows // PIECES
    gets = (core == 1) & (me < count - 1)
    gives = (core == 0) & (me > 0)
    right, left = lax.rem(me + 1, count), lax.rem(me + count - 1, count)
    near = jnp.where(core == 1, right, left)
    zero_row = 3 * rows

    def remote(src, dst, sent, got, target):
        return pltpu.make_async_remote_copy(
            src_ref=src, dst_ref=dst, send_sem=sent, recv_sem=got,
            device_id={"row": target}, device_id_type=MESH)

    def load(q):
        return pltpu.make_async_copy(own_hbm.at[:, :, q], own.at[q], load_sem.at[q])

    def send_beside(q):
        return remote(shared.at[q], beside.at[q], beside_send.at[q], beside_recv.at[q], partner)

    def send_across(q, k, target):
        at = pl.ds(pl.multiple_of(k * piece, piece), piece)
        return remote(own_hbm.at[at, :, q], across.at[q, at], across_send.at[q, k], across_recv.at[q, k], target)

    def send_last(w, k, target):
        size = rows // LAST_PIECES
        at = pl.ds(k * size, size)
        return remote(shared.at[last, w, at], across_last.at[w, at],
                      last_send.at[w, k], last_recv.at[w, k], target)

    def send_tables(target):
        return (remote(pairs_hbm, far_pairs, tab_send.at[0], tab_recv.at[0], target),
                remote(live_hbm, far_live, tab_send.at[1], tab_recv.at[1], target))

    fetches = (pltpu.make_async_copy(pairs_hbm, near_pairs, tab_load.at[0]),
               pltpu.make_async_copy(live_hbm, near_live, tab_load.at[1]))

    def send_back(t, target):
        at = pl.ds(t * (pairs // RETURNS), pairs // RETURNS)
        return remote(back.at[at], back.at[at], back_send.at[t], back_recv.at[t], target)

    for q in range(slabs):
        load(q).start()
    for fetch in fetches:
        fetch.start()

    barrier = pltpu.get_barrier_semaphore()
    hops = [me ^ (1 << r) for r in range(1, rounds)]
    for p in (partner, near):
        pl.semaphore_signal(barrier, inc=1, device_id={"row": p}, device_id_type=MESH)

    @pl.when(core == 1)
    def _():
        for p in hops:
            pl.semaphore_signal(barrier, inc=1, device_id={"row": p}, device_id_type=MESH)

    pl.semaphore_wait(barrier, 2 + core * len(hops))

    @pl.when(gives)
    def _():
        for copy in send_tables(left):
            copy.start()

        @pl.loop(0, last)
        def _(q):
            for k in range(PIECES):
                send_across(q, k, left).start()

    acc[...] = jnp.zeros_like(acc)
    for h in range(2):
        white[h, pl.ds(zero_row, 8)] = jnp.zeros((8,) + white.shape[2:], jnp.float32)

    for q in range(slabs):
        load(q).wait()

        def step(i, total):
            block = own[q, pl.ds(pl.multiple_of(i * 8, 8), 8)].astype(jnp.float32)
            return total + jnp.sum(block, axis=0)

        total = lax.fori_loop(0, rows // 8, step, jnp.zeros((windows, 16, LANES), jnp.float32))
        sums[pl.ds(q * span, span), :] = total.reshape(span, LANES)

    def hand_over():
        return remote(sums, handed, sum_send.at[0], sum_recv.at[0], partner)

    def hop(r):
        return remote(red.at[r], heard.at[r], sum_send.at[r + 1], sum_recv.at[r + 1], hops[r])

    def hand_back():
        return remote(red.at[rounds - 1], handed, sum_send.at[rounds], sum_recv.at[rounds], partner)

    @pl.when(core == 0)
    def _():
        hand_over().start()

    shifts = lax.broadcasted_iota(jnp.int32, (LANES, LAGS), 1) + (2 * bins - LAGS // 2)
    phase = lax.rem(lax.broadcasted_iota(jnp.int32, (LANES, LAGS), 0) * shifts, 2 * bins)
    angle = phase.astype(jnp.float32) * (math.pi / bins)
    base[0] = jnp.cos(angle)
    base[1] = jnp.sin(angle)

    @pl.when(core == 1)
    def _():
        hand_over().wait_recv()
        red[0] = sums[...] + handed[...]
        hop(0).start()

    tiles = bins // LANES
    shift_row = lax.broadcasted_iota(jnp.int32, (tiles, LAGS), 1) + (2 * bins - LAGS // 2)
    turns = lax.rem(lax.broadcasted_iota(jnp.int32, (tiles, LAGS), 0) * shift_row, 2 * bins)
    turned = lax.rem(turns * LANES, 2 * bins).astype(jnp.float32) * (math.pi / bins)
    turn[0] = jnp.cos(turned)
    turn[1] = jnp.sin(turned)

    for r in range(rounds - 1):
        @pl.loop(r * slabs // (rounds - 1), (r + 1) * slabs // (rounds - 1))
        def _(q):
            @pl.loop(0, 8)
            def _(f):
                ch = turn[0, pl.ds(q * 8 + f, 1), :]
                sh = turn[1, pl.ds(q * 8 + f, 1), :]

                @pl.loop(0, LANES // 16)
                def _(k):
                    at = pl.ds(pl.multiple_of(k * 16, 16), 16)
                    to = pl.ds(pl.multiple_of(f * LANES + k * 16, 16), 16)
                    bc, bs = base[0, at, :], base[1, at, :]
                    lag[q, 0, to, :] = (bc * ch - bs * sh).astype(jnp.bfloat16)
                    lag[q, 1, to, :] = (-(bs * ch + bc * sh)).astype(jnp.bfloat16)

        @pl.when(core == 1)
        def _():
            hop(r).wait_recv()
            red[r + 1] = red[r] + heard[r]
            if r + 2 < rounds:
                hop(r + 1).start()
            else:
                hand_back().start()

    def place(index, regions):
        slot = jnp.full_like(index, zero_row)
        for device, start in regions:
            offset = index - device * rows
            slot = jnp.where((offset >= 0) & (offset < rows), offset + start, slot)
        return slot

    for fetch in fetches:
        fetch.wait()
    first, second, live = near_pairs[0:1], near_pairs[1:2], near_live[...]
    far_device = jnp.where(gets, me + 1, -2)
    regions = ((me, 0), (partner, rows), (far_device, 2 * rows))
    tab_v[0] = jnp.where(live > 0, place(first, regions), zero_row)
    tab_v[1] = place(second, regions)

    @pl.when(gets)
    def _():
        for copy in send_tables(right):
            copy.wait_recv()
        tab_v[2] = jnp.where(far_live[...] > 0, place(far_pairs[0:1], ((me + 1, 2 * rows),)), zero_row)
        tab_v[3] = place(far_pairs[1:2], ((me, 0),))

    @pl.when(jnp.logical_not(gets))
    def _():
        tab_v[2] = jnp.full((1, pairs), zero_row, jnp.int32)
        tab_v[3] = jnp.full((1, pairs), zero_row, jnp.int32)

    tables = (tab_a0, tab_b0, tab_a1, tab_b1)
    moves = [pltpu.make_async_copy(tab_v.at[i], table, smem_sem.at[i]) for i, table in enumerate(tables)]
    for move in moves:
        move.start()

    def set_common(total):
        for r in range(2):
            strided = total[pl.ds(r, slabs * windows * 8, stride=2), :] * (1.0 / channels)
            common[r] = strided.reshape(slabs, windows * 8, LANES)

    @pl.when(core == 1)
    def _():
        set_common(red.at[rounds - 1])

    @pl.when(core == 0)
    def _():
        hand_back().wait_recv()
        set_common(handed)

    for move in moves:
        move.wait()

    lane_r = lax.broadcasted_iota(jnp.int32, (LANES, LANES), 0) // BAND
    lane_c = lax.broadcasted_iota(jnp.int32, (LANES, LANES), 1) // BAND
    same = (lane_r == lane_c).astype(jnp.float32).astype(jnp.bfloat16)
    depth = windows * 8

    def whiten(q, source, i, size, start, keep):
        at = pl.ds(pl.multiple_of(i * size, size), size)
        spread[0 : size * span] = source[q, at].astype(jnp.float32).reshape(size * span, LANES)
        re = spread[pl.ds(0, size * depth, stride=2), :].reshape(size, depth, LANES) - common[0, q][None]
        im = spread[pl.ds(1, size * depth, stride=2), :].reshape(size, depth, LANES) - common[1, q][None]
        power = (re * re + im * im).reshape(size * depth, LANES)
        mag = power * lax.rsqrt(jnp.maximum(power, 1e-30))
        hi = mag.astype(jnp.bfloat16)
        lo = (mag - hi.astype(jnp.float32)).astype(jnp.bfloat16)
        level = jnp.dot(hi, same, preferred_element_type=jnp.float32)
        level += jnp.dot(lo, same, preferred_element_type=jnp.float32)
        scale = (1.0 / (level * (1.0 / BAND) + 1e-06)).reshape(size, depth, LANES)
        to = pl.ds(pl.multiple_of(start + i * size, 8), size)
        for r, part in enumerate((re, im)):
            rounded = (part * scale).astype(jnp.bfloat16)
            if keep:
                for w in range(windows):
                    shared[q, w, at, r] = rounded[:, w * 8 : (w + 1) * 8]
            wide = rounded.astype(jnp.float32).reshape(size, windows, 8, LANES)
            white[lax.rem(q, 2), to, r * windows : (r + 1) * windows] = wide

    def whiten_own(q):
        @pl.loop(0, rows // WHITEN_ROWS)
        def _(i):
            whiten(q, own, i, WHITEN_ROWS, 0, True)

        send_beside(q).start()

    def expand(q):
        @pl.loop(0, rows // 16)
        def _(i):
            at = pl.ds(pl.multiple_of(i * 16, 16), 16)
            to = pl.ds(pl.multiple_of(rows + i * 16, 16), 16)
            for w in range(windows):
                wide = beside[q, w, at].astype(jnp.float32)
                white[lax.rem(q, 2), to, w] = wide[:, 0]
                white[lax.rem(q, 2), to, windows + w] = wide[:, 1]

    def expand_last(w, k):
        size = rows // LAST_PIECES
        wide = across_last[w, k * size : (k + 1) * size].astype(jnp.float32)
        to = slice(2 * rows + k * size, 2 * rows + (k + 1) * size)
        white[last % 2, to, w] = wide[:, 0]
        white[last % 2, to, windows + w] = wide[:, 1]

    def correlate(group, q, tile, after=None, used=tuple(range(windows))):
        table_a, table_b = tables[2 * group], tables[2 * group + 1]
        source = white.at[lax.rem(q, 2)]
        for t in range(pairs // tile):
            @pl.loop(0, tile // UNROLL)
            def _(i, t=t):
                at = pl.multiple_of(i * UNROLL * 8, 64)
                for u in range(UNROLL):
                    p = t * tile + i * UNROLL + u
                    a, b = source.at[table_a[0, p]], source.at[table_b[0, p]]
                    cross_re, cross_im = None, None
                    for w in used:
                        ar, ai, br, bi = a[w], a[windows + w], b[w], b[windows + w]
                        part_re, part_im = ar * br + ai * bi, ai * br - ar * bi
                        cross_re = part_re if cross_re is None else cross_re + part_re
                        cross_im = part_im if cross_im is None else cross_im + part_im
                    to = pl.ds(at + (u // 8) * 64 + u % 8, 8, stride=8)
                    planes[0, to, :] = cross_re
                    planes[1, to, :] = cross_im

            total = None
            for r in range(2):
                plane = planes[r, 0 : tile * 8].reshape(tile // 8, 8, 8, LANES)
                cross = [plane[:, f].reshape(tile, LANES).astype(jnp.bfloat16) for f in range(8)]
                part = jnp.dot(jnp.concatenate(cross, axis=1), lag[q, r], preferred_element_type=jnp.float32)
                total = part if total is None else total + part
            if after is None:
                acc[group, t * tile : (t + 1) * tile] += total
            else:
                after(t, acc[group, t * tile : (t + 1) * tile] + total)

    def give_back(t, total):
        tile = pairs // RETURNS
        back[t * tile : (t + 1) * tile] = total.astype(jnp.bfloat16)
        send_back(t, right).start()

    whiten_own(0)

    @pl.loop(0, slabs)
    def _(q):
        @pl.when(q < slabs - 1)
        def _():
            whiten_own(q + 1)

        @pl.when(gives & (q == last - 1))
        def _():
            for w in range(windows):
                for k in range(LAST_PIECES):
                    send_last(w, k, left).start()

        send_beside(q).wait_recv()
        expand(q)

        @pl.when(gets)
        def _():
            @pl.when(q < last)
            def _():
                @pl.loop(0, PIECES)
                def _(k):
                    send_across(q, k, right).wait_recv()
                    whiten(q, across, 2 * k, piece // 2, 2 * rows, False)
                    whiten(q, across, 2 * k + 1, piece // 2, 2 * rows, False)

                correlate(1, q, pairs)

            @pl.when(q == last)
            def _():
                for w in range(windows):
                    for k in range(LAST_PIECES):
                        send_last(w, k, right).wait_recv()
                        expand_last(w, k)
                    if w < windows - 1:
                        correlate(1, q, pairs, None, (w,))
                    else:
                        correlate(1, q, pairs // RETURNS, give_back, (w,))

        correlate(0, q, pairs)

    out_ref[...] = acc[0] * norm_factor

    @pl.when(gives)
    def _():
        for t in range(RETURNS):
            send_back(t, left).wait_recv()
            at = pl.ds(t * (pairs // RETURNS), pairs // RETURNS)
            out_ref[at] = out_ref[at] + back[at].astype(jnp.float32) * norm_factor

    for q in range(slabs):
        send_beside(q).wait_send()

    @pl.when(core == 0)
    def _():
        hand_over().wait_send()

    @pl.when(core == 1)
    def _():
        for r in range(rounds - 1):
            hop(r).wait_send()
        hand_back().wait_send()

    @pl.when(gives)
    def _():
        for copy in send_tables(left):
            copy.wait_send()

        @pl.loop(0, last)
        def _(q):
            for k in range(PIECES):
                send_across(q, k, left).wait_send()
        for w in range(windows):
            for k in range(LAST_PIECES):
                send_last(w, k, left).wait_send()

    @pl.when(gets)
    def _():
        for t in range(RETURNS):
            send_back(t, right).wait_send()


def body(spectra, pair_channels, pair_live):
    rows, windows, _, bins = spectra.shape
    count = lax.axis_size("row")
    slabs = bins // SLAB
    view = spectra.reshape(rows, windows, 2, bins // LANES, LANES).transpose(0, 1, 3, 2, 4)
    view = view.reshape(rows, windows, slabs, 16, LANES)
    tile_count, tile_pairs = pair_live.shape
    pairs = tile_count * tile_pairs
    index = jnp.transpose(pair_channels, (2, 0, 1)).reshape(2, pairs)
    live = pair_live.reshape(1, pairs)
    rounds = count.bit_length() - 1
    span = windows * 16
    dma = pltpu.SemaphoreType.DMA
    f32, bf16, i32 = jnp.float32, jnp.bfloat16, jnp.int32
    raw = pltpu.VMEM((slabs, rows, windows, 16, LANES), bf16)
    norm_factor = 1.0 / math.sqrt(bins * windows)
    result = pl.pallas_call(
        functools.partial(kernel, count, windows, norm_factor),
        out_shape=jax.ShapeDtypeStruct((pairs, LAGS), f32),
        in_specs=[pl.BlockSpec(memory_space=pltpu.HBM)] * 3,
        out_specs=pl.BlockSpec(memory_space=pltpu.VMEM),
        scratch_shapes=[
            raw,
            pltpu.VMEM((slabs, windows, rows, 2, 8, LANES), bf16),
            pltpu.VMEM((slabs, windows, rows, 2, 8, LANES), bf16),
            pltpu.VMEM((slabs - 1, rows, windows, 16, LANES), bf16),
            pltpu.VMEM((windows, rows, 2, 8, LANES), bf16),
            pltpu.VMEM((2, 3 * rows + 8, 2 * windows, 8, LANES), f32),
            pltpu.VMEM((WHITEN_ROWS * span, LANES), f32),
            pltpu.VMEM((2, pairs * 8, LANES), f32),
            pltpu.VMEM((slabs, 2, SLAB, LAGS), bf16),
            pltpu.VMEM((2, pairs, LAGS), f32),
            pltpu.VMEM((2, LANES, LAGS), f32),
            pltpu.VMEM((2, bins // LANES, LAGS), f32),
            pltpu.VMEM((slabs * span, LANES), f32),
            pltpu.VMEM((slabs * span, LANES), f32),
            pltpu.VMEM((rounds, slabs * span, LANES), f32),
            pltpu.VMEM((rounds - 1, slabs * span, LANES), f32),
            pltpu.VMEM((2, slabs, windows * 8, LANES), f32),
            pltpu.VMEM((2, pairs), i32),
            pltpu.VMEM((1, pairs), i32),
            pltpu.VMEM((2, pairs), i32),
            pltpu.VMEM((1, pairs), i32),
            pltpu.VMEM((4, 1, pairs), i32),
            pltpu.SMEM((1, pairs), i32), pltpu.SMEM((1, pairs), i32),
            pltpu.SMEM((1, pairs), i32), pltpu.SMEM((1, pairs), i32),
            pltpu.VMEM((pairs, LAGS), bf16),
            dma((slabs,)), dma((slabs,)), dma((slabs,)), dma((slabs - 1, PIECES)), dma((slabs - 1, PIECES)),
            dma((windows, LAST_PIECES)), dma((windows, LAST_PIECES)),
            dma((rounds + 1,)), dma((rounds + 1,)), dma((2,)), dma((2,)), dma((2,)), dma((RETURNS,)), dma((RETURNS,)), dma((4,)),
        ],
        compiler_params=pltpu.CompilerParams(
            collective_id=0, has_side_effects=True, vmem_limit_bytes=50 * 2**20),
    )(view, *(pltpu.with_memory_space_constraint(table, pltpu.HBM) for table in (index, live)))
    return result.reshape(tile_count, tile_pairs, LAGS)


def solution(mesh):
    placed = (P(("day", "row"), None, None, None), P("row", None, None), P("row", None))
    return jax.shard_map(
        body, mesh=mesh, in_specs=placed, out_specs=P(("day", "row"), None, None), check_vma=False
    )
```

```python
import functools
import math

import jax
import jax.numpy as jnp
from jax import lax
from jax.experimental import pallas as pl
from jax.experimental.pallas import tpu as pltpu
from jax.sharding import PartitionSpec as P

BAND = 64
LAGS = 512
LANES = 128
SLAB = 8 * LANES
PIECES = 2
LAST_PIECES = 2
WHITEN_ROWS = 64
UNROLL = 32
RETURNS = 2
MESH = pl.DeviceIdType.MESH


def kernel(count, windows, norm_factor, own_hbm, pairs_hbm, live_hbm, out_ref,
           own, shared, beside, across, across_last, white, spread, planes, lag, acc, base, turn,
           sums, handed, red, heard, common,
           near_pairs, near_live, far_pairs, far_live, tab_v, tab_a0, tab_b0, tab_a1, tab_b1, back,
           load_sem, beside_send, beside_recv, across_send, across_recv, last_send, last_recv, sum_send, sum_recv,
           tab_load, tab_send, tab_recv, back_send, back_recv, smem_sem):
    slabs, rows = own.shape[:2]
    span = windows * 16
    bins = slabs * SLAB
    pairs = out_ref.shape[0]
    me = lax.axis_index("row")
    core = lax.rem(me, 2)
    partner = me + 1 - 2 * core
    rounds = count.bit_length() - 1
    last = slabs - 1
    channels = count * rows
    piece = rows // PIECES
    gets = (core == 1) & (me < count - 1)
    gives = (core == 0) & (me > 0)
    right, left = lax.rem(me + 1, count), lax.rem(me + count - 1, count)
    near = jnp.where(core == 1, right, left)
    zero_row = 3 * rows

    def remote(src, dst, sent, got, target):
        return pltpu.make_async_remote_copy(
            src_ref=src, dst_ref=dst, send_sem=sent, recv_sem=got,
            device_id={"row": target}, device_id_type=MESH)

    def load(q):
        return pltpu.make_async_copy(own_hbm.at[:, :, q], own.at[q], load_sem.at[q])

    def send_beside(q):
        return remote(shared.at[q], beside.at[q], beside_send.at[q], beside_recv.at[q], partner)

    def send_across(q, k, target):
        at = pl.ds(pl.multiple_of(k * piece, piece), piece)
        return remote(own_hbm.at[at, :, q], across.at[q, at], across_send.at[q, k], across_recv.at[q, k], target)

    def send_last(w, k, target):
        size = rows // LAST_PIECES
        at = pl.ds(k * size, size)
        return remote(shared.at[last, w, at], across_last.at[w, at],
                      last_send.at[w, k], last_recv.at[w, k], target)

    def send_tables(target):
        return (remote(pairs_hbm, far_pairs, tab_send.at[0], tab_recv.at[0], target),
                remote(live_hbm, far_live, tab_send.at[1], tab_recv.at[1], target))

    fetches = (pltpu.make_async_copy(pairs_hbm, near_pairs, tab_load.at[0]),
               pltpu.make_async_copy(live_hbm, near_live, tab_load.at[1]))

    def send_back(t, target):
        at = pl.ds(t * (pairs // RETURNS), pairs // RETURNS)
        return remote(back.at[at], back.at[at], back_send.at[t], back_recv.at[t], target)

    barrier = pltpu.get_barrier_semaphore()
    hops = [me ^ (1 << r) for r in range(1, rounds)]
    for p in (partner, near):
        pl.semaphore_signal(barrier, inc=1, device_id={"row": p}, device_id_type=MESH)

    @pl.when(core == 1)
    def _():
        for p in hops:
            pl.semaphore_signal(barrier, inc=1, device_id={"row": p}, device_id_type=MESH)

    for q in range(slabs):
        load(q).start()
    for fetch in fetches:
        fetch.start()
    pl.semaphore_wait(barrier, 2 + core * len(hops))

    @pl.when(gives)
    def _():
        for copy in send_tables(left):
            copy.start()

        @pl.loop(0, last)
        def _(q):
            for k in range(PIECES):
                send_across(q, k, left).start()

    acc[...] = jnp.zeros_like(acc)
    for h in range(2):
        white[h, pl.ds(zero_row, 8)] = jnp.zeros((8,) + white.shape[2:], jnp.float32)

    for q in range(slabs):
        load(q).wait()

        def step(i, total):
            block = own[q, pl.ds(pl.multiple_of(i * 8, 8), 8)].astype(jnp.float32)
            return total + jnp.sum(block, axis=0)

        total = lax.fori_loop(0, rows // 8, step, jnp.zeros((windows, 16, LANES), jnp.float32))
        sums[pl.ds(q * span, span), :] = total.reshape(span, LANES)

    def hand_over():
        return remote(sums, handed, sum_send.at[0], sum_recv.at[0], partner)

    def hop(r):
        return remote(red.at[r], heard.at[r], sum_send.at[r + 1], sum_recv.at[r + 1], hops[r])

    def hand_back():
        return remote(red.at[rounds - 1], handed, sum_send.at[rounds], sum_recv.at[rounds], partner)

    @pl.when(core == 0)
    def _():
        hand_over().start()

    shifts = lax.broadcasted_iota(jnp.int32, (LANES, LAGS), 1) + (2 * bins - LAGS // 2)
    phase = lax.rem(lax.broadcasted_iota(jnp.int32, (LANES, LAGS), 0) * shifts, 2 * bins)
    angle = phase.astype(jnp.float32) * (math.pi / bins)
    base[0] = jnp.cos(angle)
    base[1] = jnp.sin(angle)

    @pl.when(core == 1)
    def _():
        hand_over().wait_recv()
        red[0] = sums[...] + handed[...]
        hop(0).start()

    tiles = bins // LANES
    shift_row = lax.broadcasted_iota(jnp.int32, (tiles, LAGS), 1) + (2 * bins - LAGS // 2)
    turns = lax.rem(lax.broadcasted_iota(jnp.int32, (tiles, LAGS), 0) * shift_row, 2 * bins)
    turned = lax.rem(turns * LANES, 2 * bins).astype(jnp.float32) * (math.pi / bins)
    turn[0] = jnp.cos(turned)
    turn[1] = jnp.sin(turned)

    for r in range(rounds - 1):
        @pl.loop(r * slabs // (rounds - 1), (r + 1) * slabs // (rounds - 1))
        def _(q):
            @pl.loop(0, 8)
            def _(f):
                ch = turn[0, pl.ds(q * 8 + f, 1), :]
                sh = turn[1, pl.ds(q * 8 + f, 1), :]

                @pl.loop(0, LANES // 16)
                def _(k):
                    at = pl.ds(pl.multiple_of(k * 16, 16), 16)
                    to = pl.ds(pl.multiple_of(f * LANES + k * 16, 16), 16)
                    bc, bs = base[0, at, :], base[1, at, :]
                    lag[q, 0, to, :] = (bc * ch - bs * sh).astype(jnp.bfloat16)
                    lag[q, 1, to, :] = (-(bs * ch + bc * sh)).astype(jnp.bfloat16)

        @pl.when(core == 1)
        def _():
            hop(r).wait_recv()
            red[r + 1] = red[r] + heard[r]
            if r + 2 < rounds:
                hop(r + 1).start()
            else:
                hand_back().start()

    def place(index, regions):
        slot = jnp.full_like(index, zero_row)
        for device, start in regions:
            offset = index - device * rows
            slot = jnp.where((offset >= 0) & (offset < rows), offset + start, slot)
        return slot

    for fetch in fetches:
        fetch.wait()
    first, second, live = near_pairs[0:1], near_pairs[1:2], near_live[...]
    far_device = jnp.where(gets, me + 1, -2)
    regions = ((me, 0), (partner, rows), (far_device, 2 * rows))
    tab_v[0] = jnp.where(live > 0, place(first, regions), zero_row)
    tab_v[1] = place(second, regions)

    @pl.when(gets)
    def _():
        for copy in send_tables(right):
            copy.wait_recv()
        tab_v[2] = jnp.where(far_live[...] > 0, place(far_pairs[0:1], ((me + 1, 2 * rows),)), zero_row)
        tab_v[3] = place(far_pairs[1:2], ((me, 0),))

    @pl.when(jnp.logical_not(gets))
    def _():
        tab_v[2] = jnp.full((1, pairs), zero_row, jnp.int32)
        tab_v[3] = jnp.full((1, pairs), zero_row, jnp.int32)

    tables = (tab_a0, tab_b0, tab_a1, tab_b1)
    moves = [pltpu.make_async_copy(tab_v.at[i], table, smem_sem.at[i]) for i, table in enumerate(tables)]
    for move in moves:
        move.start()

    def set_common(total):
        for r in range(2):
            strided = total[pl.ds(r, slabs * windows * 8, stride=2), :] * (1.0 / channels)
            common[r] = strided.reshape(slabs, windows * 8, LANES)

    @pl.when(core == 1)
    def _():
        set_common(red.at[rounds - 1])

    @pl.when(core == 0)
    def _():
        hand_back().wait_recv()
        set_common(handed)

    for move in moves:
        move.wait()

    lane_r = lax.broadcasted_iota(jnp.int32, (LANES, LANES), 0) // BAND
    lane_c = lax.broadcasted_iota(jnp.int32, (LANES, LANES), 1) // BAND
    same = (lane_r == lane_c).astype(jnp.float32).astype(jnp.bfloat16)
    depth = windows * 8

    def whiten(q, source, i, size, start, keep):
        at = pl.ds(pl.multiple_of(i * size, size), size)
        spread[0 : size * span] = source[q, at].astype(jnp.float32).reshape(size * span, LANES)
        re = spread[pl.ds(0, size * depth, stride=2), :].reshape(size, depth, LANES) - common[0, q][None]
        im = spread[pl.ds(1, size * depth, stride=2), :].reshape(size, depth, LANES) - common[1, q][None]
        power = (re * re + im * im).reshape(size * depth, LANES)
        mag = power * lax.rsqrt(jnp.maximum(power, 1e-30))
        hi = mag.astype(jnp.bfloat16)
        lo = (mag - hi.astype(jnp.float32)).astype(jnp.bfloat16)
        level = jnp.dot(hi, same, preferred_element_type=jnp.float32)
        level += jnp.dot(lo, same, preferred_element_type=jnp.float32)
        scale = (1.0 / (level * (1.0 / BAND) + 1e-06)).reshape(size, depth, LANES)
        to = pl.ds(pl.multiple_of(start + i * size, 8), size)
        for r, part in enumerate((re, im)):
            rounded = (part * scale).astype(jnp.bfloat16)
            if keep:
                for w in range(windows):
                    shared[q, w, at, r] = rounded[:, w * 8 : (w + 1) * 8]
            wide = rounded.astype(jnp.float32).reshape(size, windows, 8, LANES)
            white[lax.rem(q, 2), to, r * windows : (r + 1) * windows] = wide

    def whiten_own(q):
        @pl.loop(0, rows // WHITEN_ROWS)
        def _(i):
            whiten(q, own, i, WHITEN_ROWS, 0, True)

        send_beside(q).start()

    def expand(q):
        @pl.loop(0, rows // 16)
        def _(i):
            at = pl.ds(pl.multiple_of(i * 16, 16), 16)
            to = pl.ds(pl.multiple_of(rows + i * 16, 16), 16)
            for w in range(windows):
                wide = beside[q, w, at].astype(jnp.float32)
                white[lax.rem(q, 2), to, w] = wide[:, 0]
                white[lax.rem(q, 2), to, windows + w] = wide[:, 1]

    def expand_last(w, k):
        size = rows // LAST_PIECES
        wide = across_last[w, k * size : (k + 1) * size].astype(jnp.float32)
        to = slice(2 * rows + k * size, 2 * rows + (k + 1) * size)
        white[last % 2, to, w] = wide[:, 0]
        white[last % 2, to, windows + w] = wide[:, 1]

    def correlate(group, q, tile, after=None, used=tuple(range(windows))):
        table_a, table_b = tables[2 * group], tables[2 * group + 1]
        source = white.at[lax.rem(q, 2)]
        for t in range(pairs // tile):
            @pl.loop(0, tile // UNROLL)
            def _(i, t=t):
                at = pl.multiple_of(i * UNROLL * 8, 64)
                for u in range(UNROLL):
                    p = t * tile + i * UNROLL + u
                    a, b = source.at[table_a[0, p]], source.at[table_b[0, p]]
                    cross_re, cross_im = None, None
                    for w in used:
                        ar, ai, br, bi = a[w], a[windows + w], b[w], b[windows + w]
                        part_re, part_im = ar * br + ai * bi, ai * br - ar * bi
                        cross_re = part_re if cross_re is None else cross_re + part_re
                        cross_im = part_im if cross_im is None else cross_im + part_im
                    to = pl.ds(at + (u // 8) * 64 + u % 8, 8, stride=8)
                    planes[0, to, :] = cross_re
                    planes[1, to, :] = cross_im

            total = None
            for r in range(2):
                plane = planes[r, 0 : tile * 8].reshape(tile // 8, 8, 8, LANES)
                cross = [plane[:, f].reshape(tile, LANES).astype(jnp.bfloat16) for f in range(8)]
                part = jnp.dot(jnp.concatenate(cross, axis=1), lag[q, r], preferred_element_type=jnp.float32)
                total = part if total is None else total + part
            if after is None:
                acc[group, t * tile : (t + 1) * tile] += total
            else:
                after(t, acc[group, t * tile : (t + 1) * tile] + total)

    def give_back(t, total):
        tile = pairs // RETURNS
        back[t * tile : (t + 1) * tile] = total.astype(jnp.bfloat16)
        send_back(t, right).start()

    whiten_own(0)

    @pl.loop(0, slabs)
    def _(q):
        @pl.when(q < slabs - 1)
        def _():
            whiten_own(q + 1)

        @pl.when(gives & (q == last - 1))
        def _():
            for w in range(windows):
                for k in range(LAST_PIECES):
                    send_last(w, k, left).start()

        send_beside(q).wait_recv()
        expand(q)

        @pl.when(gets)
        def _():
            @pl.when(q < last)
            def _():
                @pl.loop(0, PIECES)
                def _(k):
                    send_across(q, k, right).wait_recv()
                    whiten(q, across, k, piece, 2 * rows, False)

                correlate(1, q, pairs)

            @pl.when(q == last)
            def _():
                for w in range(windows):
                    for k in range(LAST_PIECES):
                        send_last(w, k, right).wait_recv()
                        expand_last(w, k)
                    if w < windows - 1:
                        correlate(1, q, pairs, None, (w,))
                    else:
                        correlate(1, q, pairs // RETURNS, give_back, (w,))

        correlate(0, q, pairs)

    out_ref[...] = acc[0] * norm_factor

    @pl.when(gives)
    def _():
        for t in range(RETURNS):
            send_back(t, left).wait_recv()
            at = pl.ds(t * (pairs // RETURNS), pairs // RETURNS)
            out_ref[at] = out_ref[at] + back[at].astype(jnp.float32) * norm_factor

    for q in range(slabs):
        send_beside(q).wait_send()

    @pl.when(core == 0)
    def _():
        hand_over().wait_send()

    @pl.when(core == 1)
    def _():
        for r in range(rounds - 1):
            hop(r).wait_send()
        hand_back().wait_send()

    @pl.when(gives)
    def _():
        for copy in send_tables(left):
            copy.wait_send()

        @pl.loop(0, last)
        def _(q):
            for k in range(PIECES):
                send_across(q, k, left).wait_send()
        for w in range(windows):
            for k in range(LAST_PIECES):
                send_last(w, k, left).wait_send()

    @pl.when(gets)
    def _():
        for t in range(RETURNS):
            send_back(t, right).wait_send()


def body(spectra, pair_channels, pair_live):
    rows, windows, _, bins = spectra.shape
    count = lax.axis_size("row")
    slabs = bins // SLAB
    view = spectra.reshape(rows, windows, 2, bins // LANES, LANES).transpose(0, 1, 3, 2, 4)
    view = view.reshape(rows, windows, slabs, 16, LANES)
    tile_count, tile_pairs = pair_live.shape
    pairs = tile_count * tile_pairs
    index = jnp.transpose(pair_channels, (2, 0, 1)).reshape(2, pairs)
    live = pair_live.reshape(1, pairs)
    rounds = count.bit_length() - 1
    span = windows * 16
    dma = pltpu.SemaphoreType.DMA
    f32, bf16, i32 = jnp.float32, jnp.bfloat16, jnp.int32
    raw = pltpu.VMEM((slabs, rows, windows, 16, LANES), bf16)
    norm_factor = 1.0 / math.sqrt(bins * windows)
    result = pl.pallas_call(
        functools.partial(kernel, count, windows, norm_factor),
        out_shape=jax.ShapeDtypeStruct((pairs, LAGS), f32),
        in_specs=[pl.BlockSpec(memory_space=pltpu.HBM)] * 3,
        out_specs=pl.BlockSpec(memory_space=pltpu.VMEM),
        scratch_shapes=[
            raw,
            pltpu.VMEM((slabs, windows, rows, 2, 8, LANES), bf16),
            pltpu.VMEM((slabs, windows, rows, 2, 8, LANES), bf16),
            pltpu.VMEM((slabs - 1, rows, windows, 16, LANES), bf16),
            pltpu.VMEM((windows, rows, 2, 8, LANES), bf16),
            pltpu.VMEM((2, 3 * rows + 8, 2 * windows, 8, LANES), f32),
            pltpu.VMEM((WHITEN_ROWS * span, LANES), f32),
            pltpu.VMEM((2, pairs * 8, LANES), f32),
            pltpu.VMEM((slabs, 2, SLAB, LAGS), bf16),
            pltpu.VMEM((2, pairs, LAGS), f32),
            pltpu.VMEM((2, LANES, LAGS), f32),
            pltpu.VMEM((2, bins // LANES, LAGS), f32),
            pltpu.VMEM((slabs * span, LANES), f32),
            pltpu.VMEM((slabs * span, LANES), f32),
            pltpu.VMEM((rounds, slabs * span, LANES), f32),
            pltpu.VMEM((rounds - 1, slabs * span, LANES), f32),
            pltpu.VMEM((2, slabs, windows * 8, LANES), f32),
            pltpu.VMEM((2, pairs), i32),
            pltpu.VMEM((1, pairs), i32),
            pltpu.VMEM((2, pairs), i32),
            pltpu.VMEM((1, pairs), i32),
            pltpu.VMEM((4, 1, pairs), i32),
            pltpu.SMEM((1, pairs), i32), pltpu.SMEM((1, pairs), i32),
            pltpu.SMEM((1, pairs), i32), pltpu.SMEM((1, pairs), i32),
            pltpu.VMEM((pairs, LAGS), bf16),
            dma((slabs,)), dma((slabs,)), dma((slabs,)), dma((slabs - 1, PIECES)), dma((slabs - 1, PIECES)),
            dma((windows, LAST_PIECES)), dma((windows, LAST_PIECES)),
            dma((rounds + 1,)), dma((rounds + 1,)), dma((2,)), dma((2,)), dma((2,)), dma((RETURNS,)), dma((RETURNS,)), dma((4,)),
        ],
        compiler_params=pltpu.CompilerParams(
            collective_id=0, has_side_effects=True, vmem_limit_bytes=50 * 2**20),
    )(view, *(pltpu.with_memory_space_constraint(table, pltpu.HBM) for table in (index, live)))
    return result.reshape(tile_count, tile_pairs, LAGS)


def solution(mesh):
    placed = (P(("day", "row"), None, None, None), P("row", None, None), P("row", None))
    return jax.shard_map(
        body, mesh=mesh, in_specs=placed, out_specs=P(("day", "row"), None, None), check_vma=False
    )
```
